128 devices in a mesh: pipe: 8 (over y, core), seq: 16 (over z, x).
Axes of the slice: x: 4, y: 4, z: 4, core: 2. Of those that a mesh axis runs over, the one named last changes fastest.
Arguments:
- hidden: bfloat16 [2, 384, 3072], P(None, 'seq'), may hold values from -8 to 8
- mod_shift: float32 [8, 3072], P('pipe'), may hold values from -0.3 to 0.3
- mod_scale: float32 [8, 3072], P('pipe'), may hold values from -3 to 3
- mod_gate: float32 [8, 3072], P('pipe'), may hold values from 0.5 to 2.5
- norm_gain: float32 [8, 2, 128], P('pipe'), may hold values from 0.5 to 1.5
- input_proj: bfloat16 [8, 3072, 3, 2048], P('pipe', None, None, 'seq'), may hold values from -0.109375 to 0.109375
- output_proj: bfloat16 [8, 2048, 3072], P('pipe', 'seq'), may hold values from -0.5 to 0.5
- stale_cache: bfloat16 [8, 2, 384, 2, 2048], P('pipe', None, 'seq'), may hold values from -6 to 6
Outputs:
- block_output: bfloat16 [8, 2, 384, 3072], P('pipe', None, 'seq')
- fresh_cache: bfloat16 [8, 2, 384, 2, 2048], P('pipe', None, 'seq')
The draws below stay inside these ranges and needn't reach their ends.
All inputs are finite; a program needn't handle non-finite values.
Results may differ from the reference program's by a relative error of at most 0.019.
Values may be sent and summed in bfloat16 or wider, within the bound.
A program may use at most 64 MiB of HBM per device.

```python
import math
import jax
import jax.numpy as jnp
from jax import lax

D = 3072
HS = 128
HEADS = 16
PATCHES = 2
LAYERS = 8
PATCH_TOK = 384


def shard_levels(rng, extent, shards, least, high):
    def one(position, blocks):
        heights = jax.random.uniform(jax.random.fold_in(jax.random.fold_in(rng, 6), position), (blocks,), jnp.float32, least / len(shards), high / len(shards))
        return jnp.repeat(jnp.exp(heights), extent[position] // blocks).reshape((-1,) + (1,) * (len(extent) - position - 1))

    level = one(*shards[0])
    for cut in shards[1:]:
        level = level * one(*cut)
    return level


def noise(own_key, shape, scale, limit, shards=(), held_as=jnp.bfloat16):
    loudness = shard_levels(own_key, shape, shards, -0.22, 0.18) if shards else 1.0
    values = jax.random.normal(own_key, shape, jnp.float32) * scale * loudness
    return jnp.minimum(jnp.maximum(values, -limit), limit).astype(held_as)


def setup_inputs(seed: int = 0) -> dict:
    splits = jax.random.split(jax.random.key(seed), 9)
    hidden = noise(splits[0], (PATCHES, PATCH_TOK, D), 2.0, 8.0, ((1, 16),))
    mod_shift = noise(splits[1], (LAYERS, D), 0.05, 0.3, ((0, 8),), jnp.float32)
    mod_scale = noise(splits[2], (LAYERS, D), 0.5, 3.0, ((0, 8),), jnp.float32)
    mod_gate = jnp.clip(0.5 + 2.0 * jax.random.uniform(splits[3], (LAYERS, D), jnp.float32) ** shard_levels(splits[3], (LAYERS, D), ((0, 8),), -0.2, 0.2), 0.5, 2.5)
    norm_gain = jnp.clip(1.0 + 0.1 * jax.random.normal(splits[4], (LAYERS, 2, HS), jnp.float32), 0.5, 1.5)
    input_proj = noise(splits[5], (LAYERS, D, 3, HEADS * HS), D ** -0.5, 0.109375, ((0, 8), (3, 16)))
    output_proj = noise(splits[6], (LAYERS, HEADS * HS, D), HS ** -0.5, 0.5, ((0, 8), (1, 16)))
    stale_cache = noise(splits[7], (LAYERS, PATCHES, PATCH_TOK, 2, HEADS * HS), 1.0, 6.0, ((0, 8), (2, 16)))
    return dict(hidden=hidden, mod_shift=mod_shift, mod_scale=mod_scale, mod_gate=mod_gate, norm_gain=norm_gain, input_proj=input_proj, output_proj=output_proj, stale_cache=stale_cache)


def layer_norm(values, shift_row, scale_row):
    widened = values.astype(jnp.float32)
    centered = widened - lax.optimization_barrier(jnp.mean(widened, axis=-1, keepdims=True))
    spread = lax.optimization_barrier(jnp.mean(centered * centered, axis=-1, keepdims=True))
    return (centered / jnp.sqrt(spread + 1e-06) * (1.0 + scale_row) + shift_row).astype(jnp.bfloat16)

def head_norm(values, gain_row, head_size):
    row_count = values.shape[0]
    split = values.reshape(row_count, values.shape[1] // head_size, head_size)
    square = lax.optimization_barrier(jnp.mean(split * split, axis=-1, keepdims=True))
    return (split / jnp.sqrt(square + 1e-06) * gain_row).reshape(row_count, values.shape[1]).astype(jnp.bfloat16)

def attend(queries, own_keys, own_values, far_keys, far_values, head_size):
    row_count = queries.shape[0]
    head_count = queries.shape[1] // head_size
    shaped = lambda array: array.reshape(array.shape[0], head_count, head_size).astype(jnp.float32)
    query_heads = shaped(queries)
    factor = 1.0 / math.sqrt(head_size)
    near_scores = jnp.einsum('thd,shd->hts', query_heads, shaped(own_keys)) * factor
    far_scores = jnp.einsum('thd,shd->hts', query_heads, shaped(far_keys)) * factor
    near_exp = jnp.exp(near_scores)
    far_exp = jnp.exp(far_scores)
    denominator = lax.optimization_barrier(jnp.sum(near_exp, axis=-1, keepdims=True)) + lax.optimization_barrier(jnp.sum(far_exp, axis=-1, keepdims=True))
    near_prob = (near_exp / denominator).astype(jnp.bfloat16).astype(jnp.float32)
    far_prob = (far_exp / denominator).astype(jnp.bfloat16).astype(jnp.float32)
    mixed = jnp.einsum('hts,shd->thd', near_prob, shaped(own_values)) + jnp.einsum('hts,shd->thd', far_prob, shaped(far_values))
    return mixed.reshape(row_count, head_count * head_size).astype(jnp.bfloat16)

def reference(hidden, mod_shift, mod_scale, mod_gate, norm_gain, input_proj, output_proj, stale_cache):
    channels = HEADS * HS
    current = hidden
    outputs = []
    caches = []
    for layer_index in range(LAYERS):
        weight_flat = input_proj[layer_index].reshape(D, 3 * channels)

        def run_block(block_in, far_keys, far_values):
            normed = layer_norm(block_in, mod_shift[layer_index], mod_scale[layer_index])
            projected = jnp.dot(normed, weight_flat, preferred_element_type=jnp.float32)
            queries = head_norm(projected[:, :channels], norm_gain[layer_index, 0], HS)
            fresh_keys = head_norm(projected[:, channels:2 * channels], norm_gain[layer_index, 1], HS)
            values = projected[:, 2 * channels:].astype(jnp.bfloat16)
            attended = attend(queries, fresh_keys, values, far_keys, far_values, HS)
            update = jnp.dot(attended, output_proj[layer_index], preferred_element_type=jnp.float32)
            result = (block_in.astype(jnp.float32) + mod_gate[layer_index] * update).astype(jnp.bfloat16)
            return (result, fresh_keys, values)
        stale_pair = stale_cache[layer_index, 1]
        first_out, first_keys, first_values = run_block(current[0], stale_pair[:, 0], stale_pair[:, 1])
        second_out, second_keys, second_values = run_block(current[1], first_keys, first_values)
        current = jnp.stack([first_out, second_out])
        first_pair = jnp.stack([first_keys, first_values], axis=1)
        second_pair = jnp.stack([second_keys, second_values], axis=1)
        caches.append(jnp.stack([first_pair, second_pair]))
        outputs.append(current)
    return (jnp.stack(outputs), jnp.stack(caches))
```

```python
import functools
import math

import jax
import jax.numpy as jnp
from jax import lax
from jax.experimental import pallas as pl
from jax.experimental.pallas import tpu as pltpu
from jax.sharding import PartitionSpec as P

MESH = pl.DeviceIdType.MESH
SIDE = 4


def block_kernel(
    hid, shift, scale, gate, gain, w, o, st, bo_out, fc_out,
    xp, nga, ngb, xr, sg, kv, qb, og, att, atg, xo, bob, fcs, fcb,
    s_st, r_st, s_o, r_o, s_xp, r_xp, s_xr, r_xr, s_1a, r_1a, s_1b, r_1b,
    s_2a, r_2a, s_2b, r_2b, s_at, r_at, s_fc, r_fc, s_bo, r_bo,
):
    l = lax.axis_index("pipe")
    h = lax.axis_index("seq")
    sections = lax.axis_size("pipe")
    count = lax.axis_size("seq")
    i = lax.div(h, SIDE)
    j = lax.rem(h, SIDE)
    half = w.shape[0] // 2
    rows, piece = hid.shape[2], hid.shape[3]
    group = SIDE * rows
    hs = gain.shape[1]
    factor = 1.0 / math.sqrt(hs)
    nxt = lax.rem(l + 1, sections)
    prv = lax.rem(l + sections - 1, sections)

    def send(src, dst, ssem, rsem, pipe, seq):
        pltpu.make_async_remote_copy(
            src_ref=src, dst_ref=dst, send_sem=ssem, recv_sem=rsem,
            device_id=(pipe, seq), device_id_type=MESH,
        ).start()

    def local(src, dst, sem):
        pltpu.make_async_copy(src, dst, sem).start()

    def await_bytes(region, sem):
        pltpu.make_async_copy(region, region, sem).wait()

    def other(k):
        return lax.rem(h + k, count)

    barrier = pltpu.get_barrier_semaphore()
    for k in range(1, SIDE * SIDE):
        pl.semaphore_signal(barrier, inc=1, device_id=(l, other(k)), device_id_type=MESH)
    for k in range(SIDE):
        pl.semaphore_signal(barrier, inc=1, device_id=(nxt, SIDE * i + k), device_id_type=MESH)
        pl.semaphore_signal(barrier, inc=1, device_id=(prv, SIDE * i + k), device_id_type=MESH)

    @pl.when(l == 0)
    def _():
        for p in range(2):
            local(hid.at[p], xp.at[p], r_xp.at[p])

    pl.semaphore_wait(barrier, SIDE * SIDE - 1 + 2 * SIDE)

    def send_out_proj():
        for k in range(1, SIDE * SIDE):
            t = other(k)
            col = pl.multiple_of(lax.rem(t, SIDE) * piece, 128)
            send(o.at[:, pl.ds(col, piece)], og.at[h], s_o, r_o, l, t)
        col = pl.multiple_of(j * piece, 128)
        local(o.at[:, pl.ds(col, piece)], og.at[h], r_o)

    def send_stale():
        for k in range(1, SIDE * SIDE):
            t = other(k)
            send(st.at[t], sg.at[h], s_st, r_st, l, t)
        local(st.at[h], sg.at[h], r_st)

    @pl.when(l > 0)
    def _():
        send_stale()
        send_out_proj()

    def patch(p, carry):
        await_bytes(xp.at[p], r_xp.at[p])
        x = xp[p].astype(jnp.float32)
        width = SIDE * piece
        mean = jnp.sum(jnp.sum(x, axis=0), axis=-1, keepdims=True) / width
        cen = x - mean[None]
        spread = jnp.sum(jnp.sum(cen * cen, axis=0), axis=-1, keepdims=True) / width
        inv = 1.0 / jnp.sqrt(spread + 1e-06)
        normed = (cen * inv[None] * (1.0 + scale[...]) + shift[...]).astype(jnp.bfloat16)
        nga[p, i, j, :, :piece] = normed[0]
        nga[p, i, j, :, piece:] = normed[1]
        ngb[p, j, i, :, :piece] = normed[2]
        ngb[p, j, i, :, piece:] = normed[3]
        for k in (2, 1, 3):
            jj = lax.rem(j + k, SIDE)
            ii = lax.rem(i + k, SIDE)
            send(nga.at[p, i, j], nga.at[p, i, j], s_1a.at[p], r_1a.at[p], l, SIDE * i + jj)
            send(ngb.at[p, j, i], ngb.at[p, j, i], s_1b.at[p], r_1b.at[p], l, SIDE * ii + j)
        await_bytes(nga.at[p, 0, pl.ds(0, SIDE - 1)], r_1a.at[p])
        for k in (2, 1, 3):
            ii = lax.rem(i + k, SIDE)
            send(nga.at[p, i], nga.at[p, i], s_2a.at[p], r_2a.at[p], l, SIDE * ii + j)
        await_bytes(ngb.at[p, 0, pl.ds(0, SIDE - 1)], r_1b.at[p])
        for k in (2, 1, 3):
            jj = lax.rem(j + k, SIDE)
            send(ngb.at[p, j], ngb.at[p, j], s_2b.at[p], r_2b.at[p], l, SIDE * i + jj)
        for k in range(1, SIDE):
            jj = lax.rem(j + k, SIDE)
            send(xp.at[p, jj], xr.at[p, j], s_xr.at[p], r_xr.at[p], l, SIDE * i + jj)
        local(xp.at[p, j], xr.at[p, j], r_xr.at[p])

        @pl.when((l == 0) & (p == 0))
        def _():
            send_stale()
            send_out_proj()

        @pl.when(p == 0)
        def _():
            await_bytes(sg, r_st)
            for c in range(2):
                old = sg[:, c].astype(jnp.float32).reshape(count * rows, hs)
                kv[0, c] = old.astype(jnp.bfloat16)

        await_bytes(nga.at[p, pl.ds(0, SIDE - 1)], r_2a.at[p])
        await_bytes(ngb.at[p, pl.ds(0, SIDE - 1)], r_2b.at[p])

        def project(g, c):
            left = jnp.concatenate([nga[p, g, m].astype(jnp.float32) for m in range(SIDE)], axis=0)
            right = jnp.concatenate([ngb[p, m, g].astype(jnp.float32) for m in range(SIDE)], axis=0)
            out = jnp.dot(
                left.astype(jnp.bfloat16), w[:half], preferred_element_type=jnp.float32
            ) + jnp.dot(right.astype(jnp.bfloat16), w[half:], preferred_element_type=jnp.float32)
            for c in range(2):
                part = out[:, c * hs : (c + 1) * hs]
                square = jnp.mean(part * part, axis=-1, keepdims=True)
                part = part * (1.0 / jnp.sqrt(square + 1e-06)) * gain[c : c + 1, :]
                if c == 0:
                    qb[g] = part.astype(jnp.bfloat16)
                else:
                    keys = part
            values = out[:, 2 * hs :]
            kv[p + 1, 0, pl.ds(pl.multiple_of(g * group, group), group)] = keys.astype(jnp.bfloat16)
            kv[p + 1, 1, pl.ds(pl.multiple_of(g * group, group), group)] = values.astype(jnp.bfloat16)
            fcs[p, pl.ds(g * SIDE, SIDE), 0] = keys.reshape(SIDE, rows, hs).astype(jnp.bfloat16)
            fcs[p, pl.ds(g * SIDE, SIDE), 1] = values.reshape(SIDE, rows, hs).astype(jnp.bfloat16)
            return c

        lax.fori_loop(0, SIDE, project, 0)

        def attend(g):
            q = qb[g]
            dims = (((1,), (1,)), ((), ()))
            near = lax.dot_general(q, kv[p + 1, 0], dims, preferred_element_type=jnp.float32)
            far = lax.dot_general(q, kv[p, 0], dims, preferred_element_type=jnp.float32)
            near = jnp.exp(near * factor)
            far = jnp.exp(far * factor)
            den = jnp.sum(near, axis=-1, keepdims=True) + jnp.sum(far, axis=-1, keepdims=True)
            inv = 1.0 / den
            near = (near * inv).astype(jnp.bfloat16)
            far = (far * inv).astype(jnp.bfloat16)
            mixed = jnp.dot(near, kv[p + 1, 1], preferred_element_type=jnp.float32)
            mixed = mixed + jnp.dot(far, kv[p, 1], preferred_element_type=jnp.float32)
            att[p, g] = mixed.astype(jnp.bfloat16)

        for gg in (2, 1, 3, 0):
            g = lax.rem(i + gg, SIDE)
            attend(g)
            for k in range(1 if gg == 0 else 0, SIDE):
                jj = lax.rem(j + k, SIDE)
                send(att.at[p, g], atg.at[p, h], s_at.at[p], r_at.at[p], l, SIDE * g + jj)
        local(att.at[p, i], atg.at[p, h], r_at.at[p])

        for k in range(1, SIDE * SIDE):
            t = other(k)
            send(fcs.at[p, t], fcb.at[p, h], s_fc.at[p], r_fc.at[p], l, t)
        local(fcs.at[p, h], fcb.at[p, h], r_fc.at[p])

        @pl.when(p == 0)
        def _():
            await_bytes(og, r_o)

        await_bytes(xr.at[p], r_xr.at[p])
        base = xr[p].astype(jnp.float32).reshape(group, piece)
        await_bytes(atg.at[p], r_at.at[p])
        mixed = jnp.concatenate([atg[p, m] for m in range(SIDE * SIDE)], axis=1)
        update = jnp.dot(
            mixed, og[...].reshape(SIDE * SIDE * hs, piece), preferred_element_type=jnp.float32
        )
        result = base + gate[j] * update
        xo[p] = result.reshape(SIDE, rows, piece).astype(jnp.bfloat16)

        @pl.when(l < sections - 1)
        def _():
            for k in range(SIDE):
                send(xo.at[p, k], xp.at[p, j], s_xp.at[p], r_xp.at[p], nxt, SIDE * i + k)

        for k in range(1, SIDE):
            kk = lax.rem(j + k, SIDE)
            send(xo.at[p, kk], bob.at[p, j], s_bo.at[p], r_bo.at[p], l, SIDE * i + kk)
        local(xo.at[p, j], bob.at[p, j], r_bo.at[p])
        return carry

    lax.fori_loop(0, 2, patch, 0)

    for p in range(2):
        await_bytes(fcb.at[p], r_fc.at[p])
        await_bytes(bob.at[p], r_bo.at[p])
    fc_out[...] = fcb[...]
    bo_out[...] = bob[...]
    most = pl.ds(0, SIDE * SIDE - 1)
    three = pl.ds(0, SIDE - 1)
    await_bytes(sg.at[most], s_st)
    await_bytes(og.at[most], s_o)
    for p in range(2):
        await_bytes(nga.at[p, 0, three], s_1a.at[p])
        await_bytes(ngb.at[p, 0, three], s_1b.at[p])
        await_bytes(nga.at[p, three], s_2a.at[p])
        await_bytes(ngb.at[p, three], s_2b.at[p])
        await_bytes(xr.at[p, three], s_xr.at[p])
        await_bytes(atg.at[p, most], s_at.at[p])
        await_bytes(fcb.at[p, most], s_fc.at[p])
        await_bytes(bob.at[p, three], s_bo.at[p])

    @pl.when(l < sections - 1)
    def _():
        for p in range(2):
            await_bytes(xp.at[p], s_xp.at[p])


def body(hidden, mod_shift, mod_scale, mod_gate, norm_gain, input_proj, output_proj, stale_cache):
    patches, rows, width = hidden.shape
    hs = norm_gain.shape[2]
    count = SIDE * SIDE
    piece = width // SIDE
    half = width // 2
    bf, f32 = jnp.bfloat16, jnp.float32
    hid = hidden.reshape(patches, rows, SIDE, piece).transpose(0, 2, 1, 3)
    shift = mod_shift.reshape(SIDE, 1, piece)
    scale = mod_scale.reshape(SIDE, 1, piece)
    gate = mod_gate.reshape(SIDE, 1, piece)
    w = input_proj[0].reshape(width, 3 * hs)
    st = stale_cache[0, 1].reshape(rows, 2, count, hs).transpose(2, 1, 0, 3)
    vmem = pl.BlockSpec(memory_space=pltpu.VMEM)
    one = pltpu.SemaphoreType.DMA
    pair = pltpu.SemaphoreType.DMA((2,))
    bo, fc = pl.pallas_call(
        block_kernel,
        out_shape=(
            jax.ShapeDtypeStruct((patches, SIDE, rows, piece), bf),
            jax.ShapeDtypeStruct((patches, count, 2, rows, hs), bf),
        ),
        in_specs=[vmem] * 8,
        out_specs=(vmem, vmem),
        scratch_shapes=[
            pltpu.VMEM((patches, SIDE, rows, piece), bf),
            pltpu.VMEM((patches, SIDE, SIDE, rows, half), bf),
            pltpu.VMEM((patches, SIDE, SIDE, rows, half), bf),
            pltpu.VMEM((patches, SIDE, rows, piece), bf),
            pltpu.VMEM((count, 2, rows, hs), bf),
            pltpu.VMEM((patches + 1, 2, count * rows, hs), bf),
            pltpu.VMEM((SIDE, SIDE * rows, hs), bf),
            pltpu.VMEM((count, hs, piece), bf),
            pltpu.VMEM((patches, SIDE, SIDE * rows, hs), bf),
            pltpu.VMEM((patches, count, SIDE * rows, hs), bf),
            pltpu.VMEM((patches, SIDE, rows, piece), bf),
            pltpu.VMEM((patches, SIDE, rows, piece), bf),
            pltpu.VMEM((patches, count, 2, rows, hs), bf),
            pltpu.VMEM((patches, count, 2, rows, hs), bf),
            one, one, one, one,
        ] + [pair] * 18,
        compiler_params=pltpu.CompilerParams(
            collective_id=0, has_side_effects=True, vmem_limit_bytes=56 * 1024 * 1024
        ),
    )(hid, shift, scale, gate, norm_gain[0], w, output_proj[0], st)
    outputs = bo.transpose(0, 2, 1, 3).reshape(1, patches, rows, width)
    cache = fc.transpose(0, 3, 2, 1, 4).reshape(1, patches, rows, 2, count * hs)
    return outputs, cache


def solution(mesh):
    in_specs = (
        P(None, "seq", None),
        P("pipe", None),
        P("pipe", None),
        P("pipe", None),
        P("pipe", None, None),
        P("pipe", None, None, "seq"),
        P("pipe", "seq", None),
        P("pipe", None, "seq", None, None),
    )
    out_specs = (P("pipe", None, "seq", None), P("pipe", None, "seq", None, None))
    return jax.shard_map(body, mesh=mesh, in_specs=in_specs, out_specs=out_specs, check_vma=False)
```

```python
import functools
import math

import jax
import jax.numpy as jnp
from jax import lax
from jax.experimental import pallas as pl
from jax.experimental.pallas import tpu as pltpu
from jax.sharding import PartitionSpec as P

MESH = pl.DeviceIdType.MESH
SIDE = 4


def block_kernel(
    hid, shift, scale, gate, gain, w_hbm, o, st, bo_out, fc_out,
    xp, nga, ngb, xr, sg, kv, qb, og, att, atg, xo, bob, fcs, fcb,
    s_st, r_st, s_o, r_o, s_xp, r_xp, s_xr, r_xr, s_1a, r_1a, s_1b, r_1b,
    s_2a, r_2a, s_2b, r_2b, s_at, r_at, s_fc, r_fc, s_bo, r_bo, w, s_w, go,
):
    l = lax.axis_index("pipe")
    h = lax.axis_index("seq")
    sections = lax.axis_size("pipe")
    count = lax.axis_size("seq")
    i = lax.div(h, SIDE)
    j = lax.rem(h, SIDE)
    half = w.shape[1] // 2
    rows, piece = xp.shape[2], xp.shape[3]
    group = SIDE * rows
    hs = gain.shape[1]
    factor = 1.0 / math.sqrt(hs)
    nxt = lax.rem(l + 1, sections)
    prv = lax.rem(l + sections - 1, sections)
    even = lax.rem(l, 2) == 0
    partner = l + 1 - 2 * lax.rem(l, 2)
    load_w = pltpu.make_async_copy(w_hbm, w, s_w)
    load_w.start()

    def send(src, dst, ssem, rsem, pipe, seq):
        pltpu.make_async_remote_copy(
            src_ref=src, dst_ref=dst, send_sem=ssem, recv_sem=rsem,
            device_id=(pipe, seq), device_id_type=MESH,
        ).start()

    def local(src, dst, sem):
        pltpu.make_async_copy(src, dst, sem).start()

    def await_bytes(region, sem):
        pltpu.make_async_copy(region, region, sem).wait()

    def other(k):
        return lax.rem(h + k, count)

    barrier = pltpu.get_barrier_semaphore()
    for k in range(1, SIDE * SIDE):
        pl.semaphore_signal(barrier, inc=1, device_id=(l, other(k)), device_id_type=MESH)
    for k in range(SIDE):
        pl.semaphore_signal(barrier, inc=1, device_id=(nxt, SIDE * i + k), device_id_type=MESH)
        pl.semaphore_signal(barrier, inc=1, device_id=(prv, SIDE * i + k), device_id_type=MESH)

    @pl.when(l == 0)
    def _():
        for p in range(2):
            for q in range(SIDE):
                local(hid.at[p, :, pl.ds(q * piece, piece)], xp.at[p, q], r_xp.at[p])

    pl.semaphore_wait(barrier, SIDE * SIDE - 1 + 2 * SIDE)

    def send_out_proj(first, last):
        for k in range(max(first, 1), last):
            t = other(k)
            col = pl.multiple_of(lax.rem(t, SIDE) * piece, 128)
            send(o.at[:, pl.ds(col, piece)], og.at[h], s_o, r_o, l, t)
        if first == 0:
            col = pl.multiple_of(j * piece, 128)
            local(o.at[:, pl.ds(col, piece)], og.at[h], r_o)

    def tell_partner():
        pl.semaphore_signal(go, inc=1, device_id=(partner, h), device_id_type=MESH)

    def send_stale():
        for k in range(1, SIDE * SIDE):
            t = other(k)
            send(st.at[t], sg.at[h], s_st, r_st, l, t)
        local(st.at[h], sg.at[h], r_st)

    everyone = SIDE * SIDE

    @pl.when(l > 0)
    def _():
        send_stale()

    @pl.when((l > 0) & even)
    def _():
        send_out_proj(0, everyone)
        await_bytes(og, r_o)
        tell_partner()

    @pl.when(lax.rem(l, 2) == 1)
    def _():
        pl.semaphore_wait(go, 1)
        send_out_proj(0, everyone // 2)

    def patch(p, carry):
        await_bytes(xp.at[p], r_xp.at[p])
        x = xp[p].astype(jnp.float32)
        width = SIDE * piece
        mean = jnp.sum(jnp.sum(x, axis=0), axis=-1, keepdims=True) / width
        cen = x - mean[None]
        spread = jnp.sum(jnp.sum(cen * cen, axis=0), axis=-1, keepdims=True) / width
        inv = 1.0 / jnp.sqrt(spread + 1e-06)
        normed = (cen * inv[None] * (1.0 + scale[...]) + shift[...]).astype(jnp.bfloat16)
        nga[p, i, j, :, :piece] = normed[0]
        nga[p, i, j, :, piece:] = normed[1]
        ngb[p, j, i, :, :piece] = normed[2]
        ngb[p, j, i, :, piece:] = normed[3]
        @pl.when((p == 1) & even)
        def _():
            pl.semaphore_wait(go, 1)

        for k in (2, 1, 3):
            jj = lax.rem(j + k, SIDE)
            ii = lax.rem(i + k, SIDE)
            send(nga.at[p, i, j], nga.at[p, i, j], s_1a.at[p], r_1a.at[p], l, SIDE * i + jj)
            send(ngb.at[p, j, i], ngb.at[p, j, i], s_1b.at[p], r_1b.at[p], l, SIDE * ii + j)
        await_bytes(nga.at[p, 0, pl.ds(0, SIDE - 1)], r_1a.at[p])
        for k in (2, 1, 3):
            ii = lax.rem(i + k, SIDE)
            send(nga.at[p, i], nga.at[p, i], s_2a.at[p], r_2a.at[p], l, SIDE * ii + j)
        await_bytes(ngb.at[p, 0, pl.ds(0, SIDE - 1)], r_1b.at[p])
        for k in (2, 1, 3):
            jj = lax.rem(j + k, SIDE)
            send(ngb.at[p, j], ngb.at[p, j], s_2b.at[p], r_2b.at[p], l, SIDE * i + jj)
        for k in range(1, SIDE):
            jj = lax.rem(j + k, SIDE)
            send(xp.at[p, jj], xr.at[p, j], s_xr.at[p], r_xr.at[p], l, SIDE * i + jj)
        local(xp.at[p, j], xr.at[p, j], r_xr.at[p])

        @pl.when((l == 0) & (p == 0))
        def _():
            send_stale()
            send_out_proj(0, everyone)

        @pl.when((lax.rem(l, 2) == 1) & (p == 0))
        def _():
            send_out_proj(everyone // 2, everyone)

        @pl.when(p == 0)
        def _():
            load_w.wait()
            await_bytes(sg, r_st)
            for c in range(2):
                old = sg[:, c].astype(jnp.float32).reshape(count * rows, hs)
                kv[0, c] = old.astype(jnp.bfloat16)

        await_bytes(nga.at[p, pl.ds(0, SIDE - 1)], r_2a.at[p])
        await_bytes(ngb.at[p, pl.ds(0, SIDE - 1)], r_2b.at[p])

        @pl.when((p == 0) & (lax.rem(l, 2) == 1))
        def _():
            tell_partner()

        def project(g, c):
            left = jnp.concatenate([nga[p, g, m].astype(jnp.float32) for m in range(SIDE)], axis=0)
            right = jnp.concatenate([ngb[p, m, g].astype(jnp.float32) for m in range(SIDE)], axis=0)
            first = jnp.concatenate([w[m, :half] for m in range(3)], axis=1)
            second = jnp.concatenate([w[m, half:] for m in range(3)], axis=1)
            out = jnp.dot(
                left.astype(jnp.bfloat16), first, preferred_element_type=jnp.float32
            ) + jnp.dot(right.astype(jnp.bfloat16), second, preferred_element_type=jnp.float32)
            for c in range(2):
                part = out[:, c * hs : (c + 1) * hs]
                square = jnp.mean(part * part, axis=-1, keepdims=True)
                part = part * (1.0 / jnp.sqrt(square + 1e-06)) * gain[c : c + 1, :]
                if c == 0:
                    qb[g] = part.astype(jnp.bfloat16)
                else:
                    keys = part
            values = out[:, 2 * hs :]
            kv[p + 1, 0, pl.ds(pl.multiple_of(g * group, group), group)] = keys.astype(jnp.bfloat16)
            kv[p + 1, 1, pl.ds(pl.multiple_of(g * group, group), group)] = values.astype(jnp.bfloat16)
            fcs[p, pl.ds(g * SIDE, SIDE), 0] = keys.reshape(SIDE, rows, hs).astype(jnp.bfloat16)
            fcs[p, pl.ds(g * SIDE, SIDE), 1] = values.reshape(SIDE, rows, hs).astype(jnp.bfloat16)
            return c

        lax.fori_loop(0, SIDE, project, 0)

        def attend(g):
            q = qb[g]
            dims = (((1,), (1,)), ((), ()))
            near = lax.dot_general(q, kv[p + 1, 0], dims, preferred_element_type=jnp.float32)
            far = lax.dot_general(q, kv[p, 0], dims, preferred_element_type=jnp.float32)
            near = jnp.exp(near * factor)
            far = jnp.exp(far * factor)
            den = jnp.sum(near, axis=-1, keepdims=True) + jnp.sum(far, axis=-1, keepdims=True)
            inv = 1.0 / den
            near = (near * inv).astype(jnp.bfloat16)
            far = (far * inv).astype(jnp.bfloat16)
            mixed = jnp.dot(near, kv[p + 1, 1], preferred_element_type=jnp.float32)
            mixed = mixed + jnp.dot(far, kv[p, 1], preferred_element_type=jnp.float32)
            att[p, g] = mixed.astype(jnp.bfloat16)

        for gg in (2, 1, 3, 0):
            g = lax.rem(i + gg, SIDE)
            attend(g)
            for k in range(1 if gg == 0 else 0, SIDE):
                jj = lax.rem(j + k, SIDE)
                send(att.at[p, g], atg.at[p, h], s_at.at[p], r_at.at[p], l, SIDE * g + jj)
        local(att.at[p, i], atg.at[p, h], r_at.at[p])

        for k in range(1, SIDE * SIDE):
            t = other(k)
            send(fcs.at[p, t], fcb.at[p, h], s_fc.at[p], r_fc.at[p], l, t)
        local(fcs.at[p, h], fcb.at[p, h], r_fc.at[p])

        @pl.when((p == 0) & ((l == 0) | (lax.rem(l, 2) == 1)))
        def _():
            await_bytes(og, r_o)

        @pl.when((p == 0) & (l == 0))
        def _():
            tell_partner()

        await_bytes(xr.at[p], r_xr.at[p])
        base = xr[p].astype(jnp.float32).reshape(group, piece)
        await_bytes(atg.at[p], r_at.at[p])
        mixed = jnp.concatenate([atg[p, m] for m in range(SIDE * SIDE)], axis=1)
        update = jnp.dot(
            mixed, og[...].reshape(SIDE * SIDE * hs, piece), preferred_element_type=jnp.float32
        )
        result = base + gate[j] * update
        xo[p] = result.reshape(SIDE, rows, piece).astype(jnp.bfloat16)

        @pl.when(l < sections - 1)
        def _():
            for k in range(SIDE):
                send(xo.at[p, k], xp.at[p, j], s_xp.at[p], r_xp.at[p], nxt, SIDE * i + k)

        for k in range(1, SIDE):
            kk = lax.rem(j + k, SIDE)
            send(xo.at[p, kk], bob.at[p, j], s_bo.at[p], r_bo.at[p], l, SIDE * i + kk)
        local(xo.at[p, j], bob.at[p, j], r_bo.at[p])
        return carry

    lax.fori_loop(0, 2, patch, 0)

    for p in range(2):
        await_bytes(fcb.at[p], r_fc.at[p])
        await_bytes(bob.at[p], r_bo.at[p])
    fc_out[...] = fcb[...]
    for p in range(2):
        for q in range(SIDE):
            bo_out[p, :, q * piece : (q + 1) * piece] = bob[p, q]
    most = pl.ds(0, SIDE * SIDE - 1)
    three = pl.ds(0, SIDE - 1)
    await_bytes(sg.at[most], s_st)
    await_bytes(og.at[most], s_o)
    for p in range(2):
        await_bytes(nga.at[p, 0, three], s_1a.at[p])
        await_bytes(ngb.at[p, 0, three], s_1b.at[p])
        await_bytes(nga.at[p, three], s_2a.at[p])
        await_bytes(ngb.at[p, three], s_2b.at[p])
        await_bytes(xr.at[p, three], s_xr.at[p])
        await_bytes(atg.at[p, most], s_at.at[p])
        await_bytes(fcb.at[p, most], s_fc.at[p])
        await_bytes(bob.at[p, three], s_bo.at[p])

    @pl.when(l < sections - 1)
    def _():
        for p in range(2):
            await_bytes(xp.at[p], s_xp.at[p])


def body(hidden, mod_shift, mod_scale, mod_gate, norm_gain, input_proj, output_proj, stale_cache):
    patches, rows, width = hidden.shape
    hs = norm_gain.shape[2]
    count = SIDE * SIDE
    piece = width // SIDE
    half = width // 2
    bf, f32 = jnp.bfloat16, jnp.float32
    shift = mod_shift.reshape(SIDE, 1, piece)
    scale = mod_scale.reshape(SIDE, 1, piece)
    gate = mod_gate.reshape(SIDE, 1, piece)
    w = input_proj[0].transpose(1, 0, 2)
    st = stale_cache[0, 1].reshape(rows, 2, count, hs).transpose(2, 1, 0, 3)
    vmem = pl.BlockSpec(memory_space=pltpu.VMEM)
    hbm = pl.BlockSpec(memory_space=pl.ANY)
    one = pltpu.SemaphoreType.DMA
    pair = pltpu.SemaphoreType.DMA((2,))
    bo, fc = pl.pallas_call(
        block_kernel,
        out_shape=(
            jax.ShapeDtypeStruct((patches, rows, width), bf),
            jax.ShapeDtypeStruct((patches, count, 2, rows, hs), bf),
        ),
        in_specs=[vmem] * 5 + [hbm, hbm, vmem],
        out_specs=(vmem, vmem),
        scratch_shapes=[
            pltpu.VMEM((patches, SIDE, rows, piece), bf),
            pltpu.VMEM((patches, SIDE, SIDE, rows, half), bf),
            pltpu.VMEM((patches, SIDE, SIDE, rows, half), bf),
            pltpu.VMEM((patches, SIDE, rows, piece), bf),
            pltpu.VMEM((count, 2, rows, hs), bf),
            pltpu.VMEM((patches + 1, 2, count * rows, hs), bf),
            pltpu.VMEM((SIDE, SIDE * rows, hs), bf),
            pltpu.VMEM((count, hs, piece), bf),
            pltpu.VMEM((patches, SIDE, SIDE * rows, hs), bf),
            pltpu.VMEM((patches, count, SIDE * rows, hs), bf),
            pltpu.VMEM((patches, SIDE, rows, piece), bf),
            pltpu.VMEM((patches, SIDE, rows, piece), bf),
            pltpu.VMEM((patches, count, 2, rows, hs), bf),
            pltpu.VMEM((patches, count, 2, rows, hs), bf),
            one, one, one, one,
        ] + [pair] * 18 + [
            pltpu.VMEM((3, width, hs), bf),
            one,
            pltpu.SemaphoreType.REGULAR,
        ],
        compiler_params=pltpu.CompilerParams(
            collective_id=0, has_side_effects=True, vmem_limit_bytes=56 * 1024 * 1024
        ),
    )(hidden, shift, scale, gate, norm_gain[0], w, output_proj[0], st)
    outputs = bo[None]
    cache = fc.transpose(0, 3, 2, 1, 4).reshape(1, patches, rows, 2, count * hs)
    return outputs, cache


def solution(mesh):
    in_specs = (
        P(None, "seq", None),
        P("pipe", None),
        P("pipe", None),
        P("pipe", None),
        P("pipe", None, None),
        P("pipe", None, None, "seq"),
        P("pipe", "seq", None),
        P("pipe", None, "seq", None, None),
    )
    out_specs = (P("pipe", None, "seq", None), P("pipe", None, "seq", None, None))
    return jax.shard_map(body, mesh=mesh, in_specs=in_specs, out_specs=out_specs, check_vma=False)
```

```python
import functools
import math

import jax
import jax.numpy as jnp
from jax import lax
from jax.experimental import pallas as pl
from jax.experimental.pallas import tpu as pltpu
from jax.sharding import PartitionSpec as P

MESH = pl.DeviceIdType.MESH
SIDE = 4


def block_kernel(
    hid, shift, scale, gate, gain, w_hbm, o, st, bo_out, fc_out,
    xp, nga, ngb, xr, sg, kv, qb, og, att, atg, xo, bob, fcs, fcb,
    s_st, r_st, s_o, r_o, s_xp, r_xp, s_xr, r_xr, s_1a, r_1a, s_1b, r_1b,
    s_2a, r_2a, s_2b, r_2b, s_at, r_at, s_fc, r_fc, s_bo, r_bo, w, s_w, go, pa, pb,
):
    l = lax.axis_index("pipe")
    h = lax.axis_index("seq")
    sections = lax.axis_size("pipe")
    count = lax.axis_size("seq")
    i = lax.div(h, SIDE)
    j = lax.rem(h, SIDE)
    half = w.shape[0] // 2
    rows, piece = xp.shape[2], xp.shape[3]
    group = SIDE * rows
    hs = gain.shape[1]
    factor = 1.0 / math.sqrt(hs)
    nxt = lax.rem(l + 1, sections)
    prv = lax.rem(l + sections - 1, sections)
    partner = l + 1 - 2 * lax.rem(l, 2)
    for m in range(3):
        pltpu.make_async_copy(w_hbm.at[m], w.at[:, pl.ds(m * hs, hs)], s_w).start()

    def send(src, dst, ssem, rsem, pipe, seq):
        pltpu.make_async_remote_copy(
            src_ref=src, dst_ref=dst, send_sem=ssem, recv_sem=rsem,
            device_id=(pipe, seq), device_id_type=MESH,
        ).start()

    def local(src, dst, sem):
        pltpu.make_async_copy(src, dst, sem).start()

    def await_bytes(region, sem):
        pltpu.make_async_copy(region, region, sem).wait()

    def other(k):
        return lax.rem(h + k, count)

    barrier = pltpu.get_barrier_semaphore()
    for k in range(1, SIDE * SIDE):
        pl.semaphore_signal(barrier, inc=1, device_id=(l, other(k)), device_id_type=MESH)
    for k in range(SIDE):
        pl.semaphore_signal(barrier, inc=1, device_id=(nxt, SIDE * i + k), device_id_type=MESH)
        pl.semaphore_signal(barrier, inc=1, device_id=(prv, SIDE * i + k), device_id_type=MESH)

    @pl.when(l == 0)
    def _():
        for p in range(2):
            for q in range(SIDE):
                local(hid.at[p, :, pl.ds(q * piece, piece)], xp.at[p, q], r_xp.at[p])

    pl.semaphore_wait(barrier, SIDE * SIDE - 1 + 2 * SIDE)

    def send_out_proj(first, last):
        for k in range(max(first, 1), last):
            t = other(k)
            col = pl.multiple_of(lax.rem(t, SIDE) * piece, 128)
            send(o.at[:, pl.ds(col, piece)], og.at[h], s_o, r_o, l, t)
        if first == 0:
            col = pl.multiple_of(j * piece, 128)
            local(o.at[:, pl.ds(col, piece)], og.at[h], r_o)

    def tell_partner():
        pl.semaphore_signal(go, inc=1, device_id=(partner, h), device_id_type=MESH)

    def send_stale():
        for k in range(1, SIDE * SIDE):
            t = other(k)
            send(st.at[t], sg.at[h], s_st, r_st, l, t)
        local(st.at[h], sg.at[h], r_st)

    everyone = SIDE * SIDE

    @pl.when(l > 0)
    def _():
        send_stale()

    @pl.when(l > 1)
    def _():
        send_out_proj(0, everyone)

    @pl.when(l == 1)
    def _():
        pl.semaphore_wait(go, 1)
        send_out_proj(0, everyone // 2)

    def patch(p, carry):
        await_bytes(xp.at[p], r_xp.at[p])
        x = xp[p].astype(jnp.float32)
        width = SIDE * piece
        mean = jnp.sum(jnp.sum(x, axis=0), axis=-1, keepdims=True) / width
        cen = x - mean[None]
        spread = jnp.sum(jnp.sum(cen * cen, axis=0), axis=-1, keepdims=True) / width
        inv = 1.0 / jnp.sqrt(spread + 1e-06)
        normed = (cen * inv[None] * (1.0 + scale[...]) + shift[...]).astype(jnp.bfloat16)
        nga[p, i, j, :, :piece] = normed[0]
        nga[p, i, j, :, piece:] = normed[1]
        ngb[p, j, i, :, :piece] = normed[2]
        ngb[p, j, i, :, piece:] = normed[3]
        for k in (1, 3, 2):
            jj = lax.rem(j + k, SIDE)
            ii = lax.rem(i + k, SIDE)
            send(nga.at[p, i, j], nga.at[p, i, j], s_1a.at[p], r_1a.at[p, j], l, SIDE * i + jj)
            send(ngb.at[p, j, i], ngb.at[p, j, i], s_1b.at[p], r_1b.at[p, i], l, SIDE * ii + j)

        def forward(isrc, jsrc):
            for k in (1, 3, 2):
                jj = lax.rem(j + k, SIDE)
                ii = lax.rem(i + k, SIDE)
                send(nga.at[p, i, jsrc], nga.at[p, i, jsrc], s_2a.at[p], r_2a.at[p, i], l, SIDE * ii + j)
                send(ngb.at[p, j, isrc], ngb.at[p, j, isrc], s_2b.at[p], r_2b.at[p, j], l, SIDE * i + jj)

        forward(i, j)
        for k in (1, 3, 2):
            jj = lax.rem(j + k, SIDE)
            ii = lax.rem(i + k, SIDE)
            await_bytes(nga.at[p, i, jj], r_1a.at[p, jj])
            await_bytes(ngb.at[p, j, ii], r_1b.at[p, ii])
            forward(ii, jj)
        for k in range(1, SIDE):
            jj = lax.rem(j + k, SIDE)
            send(xp.at[p, jj], xr.at[p, j], s_xr.at[p], r_xr.at[p], l, SIDE * i + jj)
        local(xp.at[p, j], xr.at[p, j], r_xr.at[p])

        @pl.when((l == 0) & (p == 0))
        def _():
            send_stale()
            send_out_proj(0, everyone)

        @pl.when((l == 1) & (p == 0))
        def _():
            send_out_proj(everyone // 2, everyone)

        @pl.when(p == 0)
        def _():
            await_bytes(w, s_w)
            await_bytes(sg, r_st)
            for c in range(2):
                old = sg[:, c].astype(jnp.float32).reshape(count * rows, hs)
                kv[0, c] = old.astype(jnp.bfloat16)

        def arrive(step, c):
            k = step + lax.div(step, 2) * (5 - 2 * step)
            ii = lax.rem(i + k, SIDE)
            jj = lax.rem(j + k, SIDE)

            @pl.when(step > 0)
            def _():
                await_bytes(nga.at[p, ii], r_2a.at[p, ii])

            left = jnp.concatenate([nga[p, ii, m].astype(jnp.float32) for m in range(SIDE)], axis=0)
            pa[ii] = jnp.dot(
                left.astype(jnp.bfloat16), w[:half], preferred_element_type=jnp.float32
            )

            @pl.when(step > 0)
            def _():
                await_bytes(ngb.at[p, jj], r_2b.at[p, jj])

            right = jnp.concatenate([ngb[p, jj, m].astype(jnp.float32) for m in range(SIDE)], axis=0)
            right = jnp.dot(
                right.astype(jnp.bfloat16), w[half:], preferred_element_type=jnp.float32
            )
            pb[jj] = right.reshape(SIDE, rows, 3 * hs)
            return c

        lax.fori_loop(0, SIDE, arrive, 0)

        def project(g, c):
            out = pa[g] + pb[:, g].reshape(group, 3 * hs)
            for c in range(2):
                part = out[:, c * hs : (c + 1) * hs]
                square = jnp.mean(part * part, axis=-1, keepdims=True)
                part = part * (1.0 / jnp.sqrt(square + 1e-06)) * gain[c : c + 1, :]
                if c == 0:
                    qb[g] = part.astype(jnp.bfloat16)
                else:
                    keys = part
            values = out[:, 2 * hs :]
            kv[p + 1, 0, pl.ds(pl.multiple_of(g * group, group), group)] = keys.astype(jnp.bfloat16)
            kv[p + 1, 1, pl.ds(pl.multiple_of(g * group, group), group)] = values.astype(jnp.bfloat16)
            fcs[p, pl.ds(g * SIDE, SIDE), 0] = keys.reshape(SIDE, rows, hs).astype(jnp.bfloat16)
            fcs[p, pl.ds(g * SIDE, SIDE), 1] = values.reshape(SIDE, rows, hs).astype(jnp.bfloat16)
            return c

        lax.fori_loop(0, SIDE, project, 0)

        def attend(g):
            q = qb[g]
            dims = (((1,), (1,)), ((), ()))
            near = lax.dot_general(q, kv[p + 1, 0], dims, preferred_element_type=jnp.float32)
            far = lax.dot_general(q, kv[p, 0], dims, preferred_element_type=jnp.float32)
            near = jnp.exp(near * factor)
            far = jnp.exp(far * factor)
            den = jnp.sum(near, axis=-1, keepdims=True) + jnp.sum(far, axis=-1, keepdims=True)
            inv = 1.0 / den
            near = (near * inv).astype(jnp.bfloat16)
            far = (far * inv).astype(jnp.bfloat16)
            mixed = jnp.dot(near, kv[p + 1, 1], preferred_element_type=jnp.float32)
            mixed = mixed + jnp.dot(far, kv[p, 1], preferred_element_type=jnp.float32)
            att[p, g] = mixed.astype(jnp.bfloat16)

        for gg in (2, 1, 3, 0):
            g = lax.rem(i + gg, SIDE)
            attend(g)
            for k in range(1 if gg == 0 else 0, SIDE):
                jj = lax.rem(j + k, SIDE)
                send(att.at[p, g], atg.at[p, h], s_at.at[p], r_at.at[p], l, SIDE * g + jj)
        local(att.at[p, i], atg.at[p, h], r_at.at[p])

        for k in range(1, SIDE * SIDE):
            t = other(k)
            send(fcs.at[p, t], fcb.at[p, h], s_fc.at[p], r_fc.at[p], l, t)
        local(fcs.at[p, h], fcb.at[p, h], r_fc.at[p])

        @pl.when(p == 0)
        def _():
            await_bytes(og, r_o)

        @pl.when((p == 0) & (l == 0))
        def _():
            tell_partner()

        await_bytes(xr.at[p], r_xr.at[p])
        base = xr[p].astype(jnp.float32).reshape(group, piece)
        await_bytes(atg.at[p], r_at.at[p])
        mixed = jnp.concatenate([atg[p, m] for m in range(SIDE * SIDE)], axis=1)
        update = jnp.dot(
            mixed, og[...].reshape(SIDE * SIDE * hs, piece), preferred_element_type=jnp.float32
        )
        result = base + gate[j] * update
        xo[p] = result.reshape(SIDE, rows, piece).astype(jnp.bfloat16)

        @pl.when(l < sections - 1)
        def _():
            for k in range(SIDE):
                send(xo.at[p, k], xp.at[p, j], s_xp.at[p], r_xp.at[p], nxt, SIDE * i + k)

        for k in range(1, SIDE):
            kk = lax.rem(j + k, SIDE)
            send(xo.at[p, kk], bob.at[p, j], s_bo.at[p], r_bo.at[p], l, SIDE * i + kk)
        local(xo.at[p, j], bob.at[p, j], r_bo.at[p])
        return carry

    lax.fori_loop(0, 2, patch, 0)

    for p in range(2):
        await_bytes(fcb.at[p], r_fc.at[p])
        await_bytes(bob.at[p], r_bo.at[p])
    fc_out[...] = fcb[...]
    for p in range(2):
        for q in range(SIDE):
            bo_out[p, :, q * piece : (q + 1) * piece] = bob[p, q]
    most = pl.ds(0, SIDE * SIDE - 1)
    three = pl.ds(0, SIDE - 1)
    await_bytes(sg.at[most], s_st)
    await_bytes(og.at[most], s_o)
    for p in range(2):
        await_bytes(nga.at[p, 0, three], s_1a.at[p])
        await_bytes(ngb.at[p, 0, three], s_1b.at[p])
        await_bytes(nga.at[p, three], s_2a.at[p])
        await_bytes(ngb.at[p, three], s_2b.at[p])
        await_bytes(xr.at[p, three], s_xr.at[p])
        await_bytes(atg.at[p, most], s_at.at[p])
        await_bytes(fcb.at[p, most], s_fc.at[p])
        await_bytes(bob.at[p, three], s_bo.at[p])

    @pl.when(l < sections - 1)
    def _():
        for p in range(2):
            await_bytes(xp.at[p], s_xp.at[p])


def body(hidden, mod_shift, mod_scale, mod_gate, norm_gain, input_proj, output_proj, stale_cache):
    patches, rows, width = hidden.shape
    hs = norm_gain.shape[2]
    count = SIDE * SIDE
    piece = width // SIDE
    half = width // 2
    bf, f32 = jnp.bfloat16, jnp.float32
    shift = mod_shift.reshape(SIDE, 1, piece)
    scale = mod_scale.reshape(SIDE, 1, piece)
    gate = mod_gate.reshape(SIDE, 1, piece)
    w = input_proj[0].transpose(1, 0, 2)
    st = stale_cache[0, 1].reshape(rows, 2, count, hs).transpose(2, 1, 0, 3)
    vmem = pl.BlockSpec(memory_space=pltpu.VMEM)
    hbm = pl.BlockSpec(memory_space=pl.ANY)
    one = pltpu.SemaphoreType.DMA
    pair = pltpu.SemaphoreType.DMA((2,))
    quad = pltpu.SemaphoreType.DMA((2, SIDE))
    bo, fc = pl.pallas_call(
        block_kernel,
        out_shape=(
            jax.ShapeDtypeStruct((patches, rows, width), bf),
            jax.ShapeDtypeStruct((patches, count, 2, rows, hs), bf),
        ),
        in_specs=[vmem] * 5 + [hbm, hbm, vmem],
        out_specs=(vmem, vmem),
        scratch_shapes=[
            pltpu.VMEM((patches, SIDE, rows, piece), bf),
            pltpu.VMEM((patches, SIDE, SIDE, rows, half), bf),
            pltpu.VMEM((patches, SIDE, SIDE, rows, half), bf),
            pltpu.VMEM((patches, SIDE, rows, piece), bf),
            pltpu.VMEM((count, 2, rows, hs), bf),
            pltpu.VMEM((patches + 1, 2, count * rows, hs), bf),
            pltpu.VMEM((SIDE, SIDE * rows, hs), bf),
            pltpu.VMEM((count, hs, piece), bf),
            pltpu.VMEM((patches, SIDE, SIDE * rows, hs), bf),
            pltpu.VMEM((patches, count, SIDE * rows, hs), bf),
            pltpu.VMEM((patches, SIDE, rows, piece), bf),
            pltpu.VMEM((patches, SIDE, rows, piece), bf),
            pltpu.VMEM((patches, count, 2, rows, hs), bf),
            pltpu.VMEM((patches, count, 2, rows, hs), bf),
            one, one, one, one,
        ] + [pair] * 4 + [pair, quad] * 4 + [pair] * 6 + [
            pltpu.VMEM((width, 3 * hs), bf),
            one,
            pltpu.SemaphoreType.REGULAR,
            pltpu.VMEM((SIDE, SIDE * rows, 3 * hs), f32),
            pltpu.VMEM((SIDE, SIDE, rows, 3 * hs), f32),
        ],
        compiler_params=pltpu.CompilerParams(
            collective_id=0, has_side_effects=True, vmem_limit_bytes=56 * 1024 * 1024
        ),
    )(hidden, shift, scale, gate, norm_gain[0], w, output_proj[0], st)
    outputs = bo[None]
    cache = fc.transpose(0, 3, 2, 1, 4).reshape(1, patches, rows, 2, count * hs)
    return outputs, cache


def solution(mesh):
    in_specs = (
        P(None, "seq", None),
        P("pipe", None),
        P("pipe", None),
        P("pipe", None),
        P("pipe", None, None),
        P("pipe", None, None, "seq"),
        P("pipe", "seq", None),
        P("pipe", None, "seq", None, None),
    )
    out_specs = (P("pipe", None, "seq", None), P("pipe", None, "seq", None, None))
    return jax.shard_map(body, mesh=mesh, in_specs=in_specs, out_specs=out_specs, check_vma=False)
```

```python
import functools
import math

import jax
import jax.numpy as jnp
from jax import lax
from jax.experimental import pallas as pl
from jax.experimental.pallas import tpu as pltpu
from jax.sharding import PartitionSpec as P

MESH = pl.DeviceIdType.MESH
SIDE = 4


def block_kernel(
    hid, shift, scale, gate, gain, w_hbm, o, st, bo_out, fc_out,
    xp, nga, ngb, xr, sg, kv, qb, og, att, atg, xo, bob, fcs, fcb,
    s_st, r_st, s_o, r_o, s_xp, r_xp, s_xr, r_xr, s_1a, r_1a, s_1b, r_1b,
    s_2a, r_2a, s_2b, r_2b, s_at, r_at, s_fc, r_fc, s_bo, r_bo, w, s_w, go, pa, pb,
    up, prs, rs, s_rs, r_rs,
):
    l = lax.axis_index("pipe")
    h = lax.axis_index("seq")
    sections = lax.axis_size("pipe")
    count = lax.axis_size("seq")
    i = lax.div(h, SIDE)
    j = lax.rem(h, SIDE)
    half = w.shape[0] // 2
    rows, piece = xp.shape[2], xp.shape[3]
    group = SIDE * rows
    hs = gain.shape[1]
    factor = 1.0 / math.sqrt(hs)
    nxt = lax.rem(l + 1, sections)
    prv = lax.rem(l + sections - 1, sections)
    odd = lax.rem(l, 2) == 1
    early = l < 2
    for m in range(3):
        pltpu.make_async_copy(w_hbm.at[m], w.at[:, pl.ds(m * hs, hs)], s_w).start()

    def send(src, dst, ssem, rsem, pipe, seq):
        pltpu.make_async_remote_copy(
            src_ref=src, dst_ref=dst, send_sem=ssem, recv_sem=rsem,
            device_id=(pipe, seq), device_id_type=MESH,
        ).start()

    def local(src, dst, sem):
        pltpu.make_async_copy(src, dst, sem).start()

    def await_bytes(region, sem):
        pltpu.make_async_copy(region, region, sem).wait()

    def other(k):
        return lax.rem(h + k, count)

    barrier = pltpu.get_barrier_semaphore()
    for k in range(1, SIDE * SIDE):
        pl.semaphore_signal(barrier, inc=1, device_id=(l, other(k)), device_id_type=MESH)
    for k in range(SIDE):
        pl.semaphore_signal(barrier, inc=1, device_id=(nxt, SIDE * i + k), device_id_type=MESH)
        pl.semaphore_signal(barrier, inc=1, device_id=(prv, SIDE * i + k), device_id_type=MESH)

    @pl.when(l == 0)
    def _():
        for p in range(2):
            for q in range(SIDE):
                local(hid.at[p, :, pl.ds(q * piece, piece)], xp.at[p, q], r_xp.at[p])

    pl.semaphore_wait(barrier, SIDE * SIDE - 1 + 2 * SIDE)

    def send_out_proj():
        for k in range(1, SIDE * SIDE):
            t = other(k)
            col = pl.multiple_of(lax.rem(t, SIDE) * piece, 128)
            send(o.at[:, pl.ds(col, piece)], og.at[h], s_o, r_o, l, t)
        col = pl.multiple_of(j * piece, 128)
        local(o.at[:, pl.ds(col, piece)], og.at[h], r_o)

    def send_stale():
        for k in range(1, SIDE * SIDE):
            t = other(k)
            send(st.at[t], sg.at[h], s_st, r_st, l, t)
        local(st.at[h], sg.at[h], r_st)

    @pl.when(l > 0)
    def _():
        send_stale()

    @pl.when(~early)
    def _():
        send_out_proj()

    def start(p):
        await_bytes(xp.at[p], r_xp.at[p])
        x = xp[p].astype(jnp.float32)
        width = SIDE * piece
        mean = jnp.sum(jnp.sum(x, axis=0), axis=-1, keepdims=True) / width
        cen = x - mean[None]
        spread = jnp.sum(jnp.sum(cen * cen, axis=0), axis=-1, keepdims=True) / width
        inv = 1.0 / jnp.sqrt(spread + 1e-06)
        normed = (cen * inv[None] * (1.0 + scale[...]) + shift[...]).astype(jnp.bfloat16)
        nga[p, i, j, :, :piece] = normed[0]
        nga[p, i, j, :, piece:] = normed[1]
        ngb[p, j, i, :, :piece] = normed[2]
        ngb[p, j, i, :, piece:] = normed[3]
        for k in (1, 3, 2):
            jj = lax.rem(j + k, SIDE)
            ii = lax.rem(i + k, SIDE)
            send(nga.at[p, i, j], nga.at[p, i, j], s_1a.at[p], r_1a.at[p, j], l, SIDE * i + jj)
            send(ngb.at[p, j, i], ngb.at[p, j, i], s_1b.at[p], r_1b.at[p, i], l, SIDE * ii + j)

        forward(p, i, j)

    def forward(p, isrc, jsrc):
        for k in (1, 3, 2):
            jj = lax.rem(j + k, SIDE)
            ii = lax.rem(i + k, SIDE)
            send(nga.at[p, i, jsrc], nga.at[p, i, jsrc], s_2a.at[p], r_2a.at[p, i], l, SIDE * ii + j)
            send(ngb.at[p, j, isrc], ngb.at[p, j, isrc], s_2b.at[p], r_2b.at[p, j], l, SIDE * i + jj)

    def relay(p):
        for k in (1, 3, 2):
            jj = lax.rem(j + k, SIDE)
            ii = lax.rem(i + k, SIDE)
            await_bytes(nga.at[p, i, jj], r_1a.at[p, jj])
            await_bytes(ngb.at[p, j, ii], r_1b.at[p, ii])
            forward(p, ii, jj)
        for k in range(1, SIDE):
            jj = lax.rem(j + k, SIDE)
            send(xp.at[p, jj], xr.at[p, j], s_xr.at[p], r_xr.at[p], l, SIDE * i + jj)
        local(xp.at[p, j], xr.at[p, j], r_xr.at[p])


    def settle():
        @pl.when(l == 0)
        def _():
            send_stale()

        @pl.when(early)
        def _():
            for k in range(1, SIDE):
                jj = lax.rem(j + k, SIDE)
                col = pl.multiple_of(jj * piece, 128)
                send(o.at[:, pl.ds(col, piece)], og.at[j], s_o, r_o, l, SIDE * i + jj)
            col = pl.multiple_of(j * piece, 128)
            local(o.at[:, pl.ds(col, piece)], og.at[j], r_o)

        await_bytes(w, s_w)
        await_bytes(sg, r_st)
        for c in range(2):
            old = sg[:, c].astype(jnp.float32).reshape(count * rows, hs)
            kv[0, c] = old.astype(jnp.bfloat16)

    def project(p):
        def arrive(step, c):
            k = step + lax.div(step, 2) * (5 - 2 * step)
            ii = lax.rem(i + k, SIDE)
            jj = lax.rem(j + k, SIDE)

            @pl.when(step > 0)
            def _():
                await_bytes(nga.at[p, ii], r_2a.at[p, ii])

            left = jnp.concatenate([nga[p, ii, m].astype(jnp.float32) for m in range(SIDE)], axis=0)
            pa[ii] = jnp.dot(
                left.astype(jnp.bfloat16), w[:half], preferred_element_type=jnp.float32
            )

            @pl.when(step > 0)
            def _():
                await_bytes(ngb.at[p, jj], r_2b.at[p, jj])

            right = jnp.concatenate([ngb[p, jj, m].astype(jnp.float32) for m in range(SIDE)], axis=0)
            right = jnp.dot(
                right.astype(jnp.bfloat16), w[half:], preferred_element_type=jnp.float32
            )
            pb[jj] = right.reshape(SIDE, rows, 3 * hs)
            return c

        lax.fori_loop(0, SIDE, arrive, 0)

        def heads(g, c):
            out = pa[g] + pb[:, g].reshape(group, 3 * hs)
            for c in range(2):
                part = out[:, c * hs : (c + 1) * hs]
                square = jnp.mean(part * part, axis=-1, keepdims=True)
                part = part * (1.0 / jnp.sqrt(square + 1e-06)) * gain[c : c + 1, :]
                if c == 0:
                    qb[g] = part.astype(jnp.bfloat16)
                else:
                    keys = part
            values = out[:, 2 * hs :]
            kv[p + 1, 0, pl.ds(pl.multiple_of(g * group, group), group)] = keys.astype(jnp.bfloat16)
            kv[p + 1, 1, pl.ds(pl.multiple_of(g * group, group), group)] = values.astype(jnp.bfloat16)
            fcs[p, pl.ds(g * SIDE, SIDE), 0] = keys.reshape(SIDE, rows, hs).astype(jnp.bfloat16)
            fcs[p, pl.ds(g * SIDE, SIDE), 1] = values.reshape(SIDE, rows, hs).astype(jnp.bfloat16)
            return c

        lax.fori_loop(0, SIDE, heads, 0)

    def attend(p):
        def one(g):
            q = qb[g]
            dims = (((1,), (1,)), ((), ()))
            near = lax.dot_general(q, kv[p + 1, 0], dims, preferred_element_type=jnp.float32)
            far = lax.dot_general(q, kv[p, 0], dims, preferred_element_type=jnp.float32)
            near = jnp.exp(near * factor)
            far = jnp.exp(far * factor)
            den = jnp.sum(near, axis=-1, keepdims=True) + jnp.sum(far, axis=-1, keepdims=True)
            inv = 1.0 / den
            near = (near * inv).astype(jnp.bfloat16)
            far = (far * inv).astype(jnp.bfloat16)
            mixed = jnp.dot(near, kv[p + 1, 1], preferred_element_type=jnp.float32)
            mixed = mixed + jnp.dot(far, kv[p, 1], preferred_element_type=jnp.float32)
            att[p, g] = mixed.astype(jnp.bfloat16)

        for gg in (2, 1, 3, 0):
            g = lax.rem(i + gg, SIDE)
            one(g)

            @pl.when(early)
            def _():
                for k in range(1, SIDE):
                    jj = lax.rem(j + k, SIDE)
                    send(att.at[p, g], atg.at[p, SIDE * j + g], s_at.at[p], r_at.at[p], l, SIDE * i + jj)
                local(att.at[p, g], atg.at[p, SIDE * j + g], r_at.at[p])

            @pl.when(~early)
            def _():
                for k in range(1 if gg == 0 else 0, SIDE):
                    jj = lax.rem(j + k, SIDE)
                    send(att.at[p, g], atg.at[p, h], s_at.at[p], r_at.at[p], l, SIDE * g + jj)
                if gg == 0:
                    local(att.at[p, g], atg.at[p, h], r_at.at[p])

    def by_heads(p):
        if p == 0:
            await_bytes(og.at[pl.ds(0, SIDE)], r_o)
        weight = og[0:SIDE].reshape(SIDE * hs, piece)
        await_bytes(atg.at[p], r_at.at[p])
        for gg in (2, 1, 3, 0):
            g = lax.rem(i + gg, SIDE)
            mixed = jnp.concatenate([atg[p, SIDE * m + g] for m in range(SIDE)], axis=1)
            part = jnp.dot(mixed, weight, preferred_element_type=jnp.float32)
            if gg == 0:
                up[...] = part
            else:
                prs[p, g] = part.astype(jnp.bfloat16)
                send(prs.at[p, g], rs.at[p, i], s_rs.at[p], r_rs.at[p], l, SIDE * g + j)
        await_bytes(rs.at[p, pl.ds(0, SIDE - 1)], r_rs.at[p])
        total = up[...]
        for gg in range(1, SIDE):
            total = total + rs[p, lax.rem(i + gg, SIDE)].astype(jnp.float32)
        up[...] = total

    def by_tokens(p):
        if p == 0:
            await_bytes(og, r_o)
        await_bytes(atg.at[p], r_at.at[p])
        mixed = jnp.concatenate([atg[p, m] for m in range(SIDE * SIDE)], axis=1)
        up[...] = jnp.dot(
            mixed, og[...].reshape(SIDE * SIDE * hs, piece), preferred_element_type=jnp.float32
        )

    def finish(p):
        await_bytes(xr.at[p], r_xr.at[p])

        @pl.when(early)
        def _():
            by_heads(p)

        @pl.when(~early)
        def _():
            by_tokens(p)

        base = xr[p].astype(jnp.float32).reshape(group, piece)
        result = base + gate[j] * up[...]
        xo[p] = result.reshape(SIDE, rows, piece).astype(jnp.bfloat16)

        @pl.when(l < sections - 1)
        def _():
            for k in range(SIDE):
                send(xo.at[p, k], xp.at[p, j], s_xp.at[p], r_xp.at[p], nxt, SIDE * i + k)

        for k in range(1, SIDE):
            kk = lax.rem(j + k, SIDE)
            send(xo.at[p, kk], bob.at[p, j], s_bo.at[p], r_bo.at[p], l, SIDE * i + kk)
        local(xo.at[p, j], bob.at[p, j], r_bo.at[p])
        for k in range(1, SIDE * SIDE):
            t = other(k)
            send(fcs.at[p, t], fcb.at[p, h], s_fc.at[p], r_fc.at[p], l, t)
        local(fcs.at[p, h], fcb.at[p, h], r_fc.at[p])

    start(0)
    relay(0)
    settle()

    @pl.when(odd)
    def _():
        pl.semaphore_signal(go, inc=1, device_id=(prv, h), device_id_type=MESH)

    project(0)

    attend(0)
    finish(0)

    @pl.when(~odd)
    def _():
        pl.semaphore_wait(go, 1)

    start(1)
    relay(1)
    project(1)
    attend(1)
    finish(1)

    for p in range(2):
        await_bytes(fcb.at[p], r_fc.at[p])
        await_bytes(bob.at[p], r_bo.at[p])
    fc_out[...] = fcb[...]
    for p in range(2):
        for q in range(SIDE):
            bo_out[p, :, q * piece : (q + 1) * piece] = bob[p, q]
    most = pl.ds(0, SIDE * SIDE - 1)
    three = pl.ds(0, SIDE - 1)
    await_bytes(sg.at[most], s_st)
    for p in range(2):
        await_bytes(nga.at[p, 0, three], s_1a.at[p])
        await_bytes(ngb.at[p, 0, three], s_1b.at[p])
        await_bytes(nga.at[p, three], s_2a.at[p])
        await_bytes(ngb.at[p, three], s_2b.at[p])
        await_bytes(xr.at[p, three], s_xr.at[p])
        await_bytes(fcb.at[p, most], s_fc.at[p])
        await_bytes(bob.at[p, three], s_bo.at[p])

    @pl.when(early)
    def _():
        await_bytes(og.at[three], s_o)
        for p in range(2):
            await_bytes(atg.at[p, pl.ds(0, SIDE * (SIDE - 1))], s_at.at[p])
            await_bytes(rs.at[p, three], s_rs.at[p])

    @pl.when(~early)
    def _():
        await_bytes(og.at[most], s_o)
        for p in range(2):
            await_bytes(atg.at[p, most], s_at.at[p])

    @pl.when(l < sections - 1)
    def _():
        for p in range(2):
            await_bytes(xp.at[p], s_xp.at[p])


def body(hidden, mod_shift, mod_scale, mod_gate, norm_gain, input_proj, output_proj, stale_cache):
    patches, rows, width = hidden.shape
    hs = norm_gain.shape[2]
    count = SIDE * SIDE
    piece = width // SIDE
    half = width // 2
    bf, f32 = jnp.bfloat16, jnp.float32
    shift = mod_shift.reshape(SIDE, 1, piece)
    scale = mod_scale.reshape(SIDE, 1, piece)
    gate = mod_gate.reshape(SIDE, 1, piece)
    w = input_proj[0].transpose(1, 0, 2)
    st = stale_cache[0, 1].reshape(rows, 2, count, hs).transpose(2, 1, 0, 3)
    vmem = pl.BlockSpec(memory_space=pltpu.VMEM)
    hbm = pl.BlockSpec(memory_space=pl.ANY)
    one = pltpu.SemaphoreType.DMA
    pair = pltpu.SemaphoreType.DMA((2,))
    quad = pltpu.SemaphoreType.DMA((2, SIDE))
    bo, fc = pl.pallas_call(
        block_kernel,
        out_shape=(
            jax.ShapeDtypeStruct((patches, rows, width), bf),
            jax.ShapeDtypeStruct((patches, count, 2, rows, hs), bf),
        ),
        in_specs=[vmem] * 5 + [hbm, hbm, vmem],
        out_specs=(vmem, vmem),
        scratch_shapes=[
            pltpu.VMEM((patches, SIDE, rows, piece), bf),
            pltpu.VMEM((patches, SIDE, SIDE, rows, half), bf),
            pltpu.VMEM((patches, SIDE, SIDE, rows, half), bf),
            pltpu.VMEM((patches, SIDE, rows, piece), bf),
            pltpu.VMEM((count, 2, rows, hs), bf),
            pltpu.VMEM((patches + 1, 2, count * rows, hs), bf),
            pltpu.VMEM((SIDE, SIDE * rows, hs), bf),
            pltpu.VMEM((count, hs, piece), bf),
            pltpu.VMEM((patches, SIDE, SIDE * rows, hs), bf),
            pltpu.VMEM((patches, count, SIDE * rows, hs), bf),
            pltpu.VMEM((patches, SIDE, rows, piece), bf),
            pltpu.VMEM((patches, SIDE, rows, piece), bf),
            pltpu.VMEM((patches, count, 2, rows, hs), bf),
            pltpu.VMEM((patches, count, 2, rows, hs), bf),
            one, one, one, one,
        ] + [pair] * 4 + [pair, quad] * 4 + [pair] * 6 + [
            pltpu.VMEM((width, 3 * hs), bf),
            one,
            pltpu.SemaphoreType.REGULAR,
            pltpu.VMEM((SIDE, SIDE * rows, 3 * hs), f32),
            pltpu.VMEM((SIDE, SIDE, rows, 3 * hs), f32),
            pltpu.VMEM((SIDE * rows, piece), f32),
            pltpu.VMEM((patches, SIDE, SIDE * rows, piece), bf),
            pltpu.VMEM((patches, SIDE, SIDE * rows, piece), bf),
            pair, pair,
        ],
        compiler_params=pltpu.CompilerParams(
            collective_id=0, has_side_effects=True, vmem_limit_bytes=56 * 1024 * 1024
        ),
    )(hidden, shift, scale, gate, norm_gain[0], w, output_proj[0], st)
    outputs = bo[None]
    cache = fc.transpose(0, 3, 2, 1, 4).reshape(1, patches, rows, 2, count * hs)
    return outputs, cache


def solution(mesh):
    in_specs = (
        P(None, "seq", None),
        P("pipe", None),
        P("pipe", None),
        P("pipe", None),
        P("pipe", None, None),
        P("pipe", None, None, "seq"),
        P("pipe", "seq", None),
        P("pipe", None, "seq", None, None),
    )
    out_specs = (P("pipe", None, "seq", None), P("pipe", None, "seq", None, None))
    return jax.shard_map(body, mesh=mesh, in_specs=in_specs, out_specs=out_specs, check_vma=False)
```

```python
import functools
import math

import jax
import jax.numpy as jnp
from jax import lax
from jax.experimental import pallas as pl
from jax.experimental.pallas import tpu as pltpu
from jax.sharding import PartitionSpec as P

MESH = pl.DeviceIdType.MESH
SIDE = 4


def block_kernel(
    hid, shift, scale, gate, gain, w_hbm, o, st, bo_out, fc_out,
    xp, nga, ngb, xr, sg, kv, qb, og, att, atg, xo, bob, fcs, fcb,
    s_st, r_st, s_o, r_o, s_xp, r_xp, s_xr, r_xr, s_1a, r_1a, s_1b, r_1b,
    s_2a, r_2a, s_2b, r_2b, s_at, r_at, s_fc, r_fc, s_bo, r_bo, w, s_w, go, pa, pb,
    up, prs, rs, s_rs, r_rs,
):
    l = lax.axis_index("pipe")
    h = lax.axis_index("seq")
    sections = lax.axis_size("pipe")
    count = lax.axis_size("seq")
    i = lax.div(h, SIDE)
    j = lax.rem(h, SIDE)
    half = w.shape[0] // 2
    rows, piece = xp.shape[2], xp.shape[3]
    group = SIDE * rows
    hs = gain.shape[1]
    factor = 1.0 / math.sqrt(hs)
    nxt = lax.rem(l + 1, sections)
    prv = lax.rem(l + sections - 1, sections)
    odd = lax.rem(l, 2) == 1
    early = l < 2
    for m in range(3):
        pltpu.make_async_copy(w_hbm.at[m], w.at[:, pl.ds(m * hs, hs)], s_w).start()

    def send(src, dst, ssem, rsem, pipe, seq):
        pltpu.make_async_remote_copy(
            src_ref=src, dst_ref=dst, send_sem=ssem, recv_sem=rsem,
            device_id=(pipe, seq), device_id_type=MESH,
        ).start()

    def local(src, dst, sem):
        pltpu.make_async_copy(src, dst, sem).start()

    def await_bytes(region, sem):
        pltpu.make_async_copy(region, region, sem).wait()

    def other(k):
        return lax.rem(h + k, count)

    barrier = pltpu.get_barrier_semaphore()
    for k in range(1, SIDE * SIDE):
        pl.semaphore_signal(barrier, inc=1, device_id=(l, other(k)), device_id_type=MESH)
    for k in range(SIDE):
        pl.semaphore_signal(barrier, inc=1, device_id=(nxt, SIDE * i + k), device_id_type=MESH)
        pl.semaphore_signal(barrier, inc=1, device_id=(prv, SIDE * i + k), device_id_type=MESH)

    @pl.when(l == 0)
    def _():
        for p in range(2):
            for q in range(SIDE):
                local(hid.at[p, :, pl.ds(q * piece, piece)], xp.at[p, q], r_xp.at[p])

    pl.semaphore_wait(barrier, SIDE * SIDE - 1 + 2 * SIDE)

    def send_out_proj():
        for k in range(1, SIDE * SIDE):
            t = other(k)
            col = pl.multiple_of(lax.rem(t, SIDE) * piece, 128)
            send(o.at[:, pl.ds(col, piece)], og.at[h], s_o, r_o, l, t)
        col = pl.multiple_of(j * piece, 128)
        local(o.at[:, pl.ds(col, piece)], og.at[h], r_o)

    def send_rows():
        for k in range(1, SIDE):
            jj = lax.rem(j + k, SIDE)
            col = pl.multiple_of(jj * piece, 128)
            send(o.at[:, pl.ds(col, piece)], og.at[j], s_o, r_o, l, SIDE * i + jj)
        col = pl.multiple_of(j * piece, 128)
        local(o.at[:, pl.ds(col, piece)], og.at[j], r_o)

    def send_stale():
        for k in range(1, SIDE * SIDE):
            t = other(k)
            send(st.at[t], sg.at[h], s_st, r_st, l, t)
        local(st.at[h], sg.at[h], r_st)

    send_stale()

    @pl.when(~early)
    def _():
        send_out_proj()

    @pl.when(l == 1)
    def _():
        pl.semaphore_wait(go, 1)
        send_rows()

    def start(p):
        await_bytes(xp.at[p], r_xp.at[p])
        x = xp[p].astype(jnp.float32)
        width = SIDE * piece
        mean = jnp.sum(jnp.sum(x, axis=0), axis=-1, keepdims=True) / width
        cen = x - mean[None]
        spread = jnp.sum(jnp.sum(cen * cen, axis=0), axis=-1, keepdims=True) / width
        inv = 1.0 / jnp.sqrt(spread + 1e-06)
        normed = (cen * inv[None] * (1.0 + scale[...]) + shift[...]).astype(jnp.bfloat16)
        nga[p, i, j, :, :piece] = normed[0]
        nga[p, i, j, :, piece:] = normed[1]
        ngb[p, j, i, :, :piece] = normed[2]
        ngb[p, j, i, :, piece:] = normed[3]
        for k in (1, 3, 2):
            jj = lax.rem(j + k, SIDE)
            ii = lax.rem(i + k, SIDE)
            send(nga.at[p, i, j], nga.at[p, i, j], s_1a.at[p], r_1a.at[p, j], l, SIDE * i + jj)
            send(ngb.at[p, j, i], ngb.at[p, j, i], s_1b.at[p], r_1b.at[p, i], l, SIDE * ii + j)

        forward(p, i, j)

    def forward(p, isrc, jsrc):
        for k in (1, 3, 2):
            jj = lax.rem(j + k, SIDE)
            ii = lax.rem(i + k, SIDE)
            send(nga.at[p, i, jsrc], nga.at[p, i, jsrc], s_2a.at[p], r_2a.at[p, i], l, SIDE * ii + j)
            send(ngb.at[p, j, isrc], ngb.at[p, j, isrc], s_2b.at[p], r_2b.at[p, j], l, SIDE * i + jj)

    def relay(p):
        for k in (1, 3, 2):
            jj = lax.rem(j + k, SIDE)
            ii = lax.rem(i + k, SIDE)
            await_bytes(nga.at[p, i, jj], r_1a.at[p, jj])
            await_bytes(ngb.at[p, j, ii], r_1b.at[p, ii])
            forward(p, ii, jj)
        for k in range(1, SIDE):
            jj = lax.rem(j + k, SIDE)
            send(xp.at[p, jj], xr.at[p, j], s_xr.at[p], r_xr.at[p], l, SIDE * i + jj)
        local(xp.at[p, j], xr.at[p, j], r_xr.at[p])


    def settle():
        @pl.when(l == 0)
        def _():
            send_rows()

        await_bytes(w, s_w)
        await_bytes(sg, r_st)
        for c in range(2):
            old = sg[:, c].astype(jnp.float32).reshape(count * rows, hs)
            kv[0, c] = old.astype(jnp.bfloat16)

    def project(p):
        def arrive(step, c):
            k = step + lax.div(step, 2) * (5 - 2 * step)
            ii = lax.rem(i + k, SIDE)
            jj = lax.rem(j + k, SIDE)

            @pl.when(step > 0)
            def _():
                await_bytes(nga.at[p, ii], r_2a.at[p, ii])

            left = jnp.concatenate([nga[p, ii, m].astype(jnp.float32) for m in range(SIDE)], axis=0)
            pa[ii] = jnp.dot(
                left.astype(jnp.bfloat16), w[:half], preferred_element_type=jnp.float32
            )

            @pl.when(step > 0)
            def _():
                await_bytes(ngb.at[p, jj], r_2b.at[p, jj])

            right = jnp.concatenate([ngb[p, jj, m].astype(jnp.float32) for m in range(SIDE)], axis=0)
            right = jnp.dot(
                right.astype(jnp.bfloat16), w[half:], preferred_element_type=jnp.float32
            )
            pb[jj] = right.reshape(SIDE, rows, 3 * hs)
            return c

        lax.fori_loop(0, SIDE, arrive, 0)

        def heads(g, c):
            out = pa[g] + pb[:, g].reshape(group, 3 * hs)
            for c in range(2):
                part = out[:, c * hs : (c + 1) * hs]
                square = jnp.mean(part * part, axis=-1, keepdims=True)
                part = part * (1.0 / jnp.sqrt(square + 1e-06)) * gain[c : c + 1, :]
                if c == 0:
                    qb[g] = part.astype(jnp.bfloat16)
                else:
                    keys = part
            values = out[:, 2 * hs :]
            kv[p + 1, 0, pl.ds(pl.multiple_of(g * group, group), group)] = keys.astype(jnp.bfloat16)
            kv[p + 1, 1, pl.ds(pl.multiple_of(g * group, group), group)] = values.astype(jnp.bfloat16)
            fcs[p, pl.ds(g * SIDE, SIDE), 0] = keys.reshape(SIDE, rows, hs).astype(jnp.bfloat16)
            fcs[p, pl.ds(g * SIDE, SIDE), 1] = values.reshape(SIDE, rows, hs).astype(jnp.bfloat16)
            return c

        lax.fori_loop(0, SIDE, heads, 0)

    def attend(p):
        def one(g):
            q = qb[g]
            dims = (((1,), (1,)), ((), ()))
            near = lax.dot_general(q, kv[p + 1, 0], dims, preferred_element_type=jnp.float32)
            far = lax.dot_general(q, kv[p, 0], dims, preferred_element_type=jnp.float32)
            near = jnp.exp(near * factor)
            far = jnp.exp(far * factor)
            den = jnp.sum(near, axis=-1, keepdims=True) + jnp.sum(far, axis=-1, keepdims=True)
            inv = 1.0 / den
            near = (near * inv).astype(jnp.bfloat16)
            far = (far * inv).astype(jnp.bfloat16)
            mixed = jnp.dot(near, kv[p + 1, 1], preferred_element_type=jnp.float32)
            mixed = mixed + jnp.dot(far, kv[p, 1], preferred_element_type=jnp.float32)
            att[p, g] = mixed.astype(jnp.bfloat16)

        for gg in (2, 1, 3, 0):
            g = lax.rem(i + gg, SIDE)
            one(g)

            @pl.when(early)
            def _():
                for k in range(1, SIDE):
                    jj = lax.rem(j + k, SIDE)
                    send(att.at[p, g], atg.at[p, SIDE * j + g], s_at.at[p], r_at.at[p], l, SIDE * i + jj)
                local(att.at[p, g], atg.at[p, SIDE * j + g], r_at.at[p])

            @pl.when(~early)
            def _():
                for k in range(1 if gg == 0 else 0, SIDE):
                    jj = lax.rem(j + k, SIDE)
                    send(att.at[p, g], atg.at[p, h], s_at.at[p], r_at.at[p], l, SIDE * g + jj)
                if gg == 0:
                    local(att.at[p, g], atg.at[p, h], r_at.at[p])

    def by_heads(p):
        if p == 0:
            await_bytes(og.at[pl.ds(0, SIDE)], r_o)
        weight = og[0:SIDE].reshape(SIDE * hs, piece)
        await_bytes(atg.at[p], r_at.at[p])
        for gg in (2, 1, 3, 0):
            g = lax.rem(i + gg, SIDE)
            mixed = jnp.concatenate([atg[p, SIDE * m + g] for m in range(SIDE)], axis=1)
            part = jnp.dot(mixed, weight, preferred_element_type=jnp.float32)
            if gg == 0:
                up[...] = part
            else:
                prs[p, g] = part.astype(jnp.bfloat16)
                send(prs.at[p, g], rs.at[p, i], s_rs.at[p], r_rs.at[p], l, SIDE * g + j)
        await_bytes(rs.at[p, pl.ds(0, SIDE - 1)], r_rs.at[p])
        total = up[...]
        for gg in range(1, SIDE):
            total = total + rs[p, lax.rem(i + gg, SIDE)].astype(jnp.float32)
        up[...] = total

    def by_tokens(p):
        if p == 0:
            await_bytes(og, r_o)
        await_bytes(atg.at[p], r_at.at[p])
        mixed = jnp.concatenate([atg[p, m] for m in range(SIDE * SIDE)], axis=1)
        up[...] = jnp.dot(
            mixed, og[...].reshape(SIDE * SIDE * hs, piece), preferred_element_type=jnp.float32
        )

    def finish(p):
        await_bytes(xr.at[p], r_xr.at[p])

        @pl.when(early)
        def _():
            by_heads(p)

        @pl.when(~early)
        def _():
            by_tokens(p)

        base = xr[p].astype(jnp.float32).reshape(group, piece)
        result = base + gate[j] * up[...]
        xo[p] = result.reshape(SIDE, rows, piece).astype(jnp.bfloat16)

        @pl.when(l < sections - 1)
        def _():
            for k in range(SIDE):
                send(xo.at[p, k], xp.at[p, j], s_xp.at[p], r_xp.at[p], nxt, SIDE * i + k)

        for k in range(1, SIDE):
            kk = lax.rem(j + k, SIDE)
            send(xo.at[p, kk], bob.at[p, j], s_bo.at[p], r_bo.at[p], l, SIDE * i + kk)
        local(xo.at[p, j], bob.at[p, j], r_bo.at[p])

    def send_cache(p):
        for k in range(1, SIDE * SIDE):
            t = other(k)
            send(fcs.at[p, t], fcb.at[p, h], s_fc.at[p], r_fc.at[p], l, t)
        local(fcs.at[p, h], fcb.at[p, h], r_fc.at[p])

    start(0)
    relay(0)
    settle()

    @pl.when(odd)
    def _():
        pl.semaphore_signal(go, inc=1, device_id=(prv, h), device_id_type=MESH)

    project(0)

    attend(0)
    finish(0)

    @pl.when(l == 0)
    def _():
        pl.semaphore_signal(go, inc=1, device_id=(nxt, h), device_id_type=MESH)


    @pl.when(~odd)
    def _():
        pl.semaphore_wait(go, 1)

    start(1)
    relay(1)
    project(1)
    attend(1)
    send_cache(0)
    finish(1)
    send_cache(1)

    for p in range(2):
        await_bytes(fcb.at[p], r_fc.at[p])
        await_bytes(bob.at[p], r_bo.at[p])
    fc_out[...] = fcb[...]
    for p in range(2):
        for q in range(SIDE):
            bo_out[p, :, q * piece : (q + 1) * piece] = bob[p, q].astype(jnp.float32)
    most = pl.ds(0, SIDE * SIDE - 1)
    three = pl.ds(0, SIDE - 1)
    await_bytes(sg.at[most], s_st)
    for p in range(2):
        await_bytes(nga.at[p, 0, three], s_1a.at[p])
        await_bytes(ngb.at[p, 0, three], s_1b.at[p])
        await_bytes(nga.at[p, three], s_2a.at[p])
        await_bytes(ngb.at[p, three], s_2b.at[p])
        await_bytes(xr.at[p, three], s_xr.at[p])
        await_bytes(fcb.at[p, most], s_fc.at[p])
        await_bytes(bob.at[p, three], s_bo.at[p])

    @pl.when(early)
    def _():
        await_bytes(og.at[three], s_o)
        for p in range(2):
            await_bytes(atg.at[p, pl.ds(0, SIDE * (SIDE - 1))], s_at.at[p])
            await_bytes(rs.at[p, three], s_rs.at[p])

    @pl.when(~early)
    def _():
        await_bytes(og.at[most], s_o)
        for p in range(2):
            await_bytes(atg.at[p, most], s_at.at[p])

    @pl.when(l < sections - 1)
    def _():
        for p in range(2):
            await_bytes(xp.at[p], s_xp.at[p])


def body(hidden, mod_shift, mod_scale, mod_gate, norm_gain, input_proj, output_proj, stale_cache):
    patches, rows, width = hidden.shape
    hs = norm_gain.shape[2]
    count = SIDE * SIDE
    piece = width // SIDE
    half = width // 2
    bf, f32 = jnp.bfloat16, jnp.float32
    shift = mod_shift.reshape(SIDE, 1, piece)
    scale = mod_scale.reshape(SIDE, 1, piece)
    gate = mod_gate.reshape(SIDE, 1, piece)
    w = input_proj[0].transpose(1, 0, 2)
    st = stale_cache[0, 1].reshape(rows, 2, count, hs).transpose(2, 1, 0, 3)
    vmem = pl.BlockSpec(memory_space=pltpu.VMEM)
    hbm = pl.BlockSpec(memory_space=pl.ANY)
    one = pltpu.SemaphoreType.DMA
    pair = pltpu.SemaphoreType.DMA((2,))
    quad = pltpu.SemaphoreType.DMA((2, SIDE))
    bo, fc = pl.pallas_call(
        block_kernel,
        out_shape=(
            jax.ShapeDtypeStruct((patches, rows, width), f32),
            jax.ShapeDtypeStruct((patches, count, 2, rows, hs), bf),
        ),
        in_specs=[vmem] * 5 + [hbm, hbm, vmem],
        out_specs=(vmem, vmem),
        scratch_shapes=[
            pltpu.VMEM((patches, SIDE, rows, piece), bf),
            pltpu.VMEM((patches, SIDE, SIDE, rows, half), bf),
            pltpu.VMEM((patches, SIDE, SIDE, rows, half), bf),
            pltpu.VMEM((patches, SIDE, rows, piece), bf),
            pltpu.VMEM((count, 2, rows, hs), bf),
            pltpu.VMEM((patches + 1, 2, count * rows, hs), bf),
            pltpu.VMEM((SIDE, SIDE * rows, hs), bf),
            pltpu.VMEM((count, hs, piece), bf),
            pltpu.VMEM((patches, SIDE, SIDE * rows, hs), bf),
            pltpu.VMEM((patches, count, SIDE * rows, hs), bf),
            pltpu.VMEM((patches, SIDE, rows, piece), bf),
            pltpu.VMEM((patches, SIDE, rows, piece), bf),
            pltpu.VMEM((patches, count, 2, rows, hs), bf),
            pltpu.VMEM((patches, count, 2, rows, hs), bf),
            one, one, one, one,
        ] + [pair] * 4 + [pair, quad] * 4 + [pair] * 6 + [
            pltpu.VMEM((width, 3 * hs), bf),
            one,
            pltpu.SemaphoreType.REGULAR,
            pltpu.VMEM((SIDE, SIDE * rows, 3 * hs), f32),
            pltpu.VMEM((SIDE, SIDE, rows, 3 * hs), f32),
            pltpu.VMEM((SIDE * rows, piece), f32),
            pltpu.VMEM((patches, SIDE, SIDE * rows, piece), bf),
            pltpu.VMEM((patches, SIDE, SIDE * rows, piece), bf),
            pair, pair,
        ],
        compiler_params=pltpu.CompilerParams(
            collective_id=0, has_side_effects=True, vmem_limit_bytes=56 * 1024 * 1024
        ),
    )(hidden, shift, scale, gate, norm_gain[0], w, output_proj[0], st)
    outputs = bo.astype(bf)[None]
    cache = fc.transpose(0, 3, 2, 1, 4).reshape(1, patches, rows, 2, count * hs)
    return outputs, cache


def solution(mesh):
    in_specs = (
        P(None, "seq", None),
        P("pipe", None),
        P("pipe", None),
        P("pipe", None),
        P("pipe", None, None),
        P("pipe", None, None, "seq"),
        P("pipe", "seq", None),
        P("pipe", None, "seq", None, None),
    )
    out_specs = (P("pipe", None, "seq", None), P("pipe", None, "seq", None, None))
    return jax.shard_map(body, mesh=mesh, in_specs=in_specs, out_specs=out_specs, check_vma=False)
```

```python
import functools
import math

import jax
import jax.numpy as jnp
from jax import lax
from jax.experimental import pallas as pl
from jax.experimental.pallas import tpu as pltpu
from jax.sharding import PartitionSpec as P

MESH = pl.DeviceIdType.MESH
SIDE = 4


def block_kernel(
    hid, shift, scale, gate, gain, w_hbm, o, st, bo_out, fc_out,
    xp, nga, ngb, xr, sg, kv, qb, og, att, atg, xo, bob, fcs, fcb,
    s_st, r_st, s_o, r_o, s_xp, r_xp, s_xr, r_xr, s_1a, r_1a, s_1b, r_1b,
    s_2a, r_2a, s_2b, r_2b, s_at, r_at, s_fc, r_fc, s_bo, r_bo, w, s_w, go, pa, pb,
    up, prs, rs, s_rs, r_rs,
):
    l = lax.axis_index("pipe")
    h = lax.axis_index("seq")
    sections = lax.axis_size("pipe")
    count = lax.axis_size("seq")
    i = lax.div(h, SIDE)
    j = lax.rem(h, SIDE)
    half = w.shape[0] // 2
    rows, piece = xp.shape[2], xp.shape[3]
    group = SIDE * rows
    hs = gain.shape[1]
    factor = 1.0 / math.sqrt(hs)
    nxt = lax.rem(l + 1, sections)
    prv = lax.rem(l + sections - 1, sections)
    odd = lax.rem(l, 2) == 1
    early = l < 2
    for m in range(3):
        pltpu.make_async_copy(w_hbm.at[m], w.at[:, pl.ds(m * hs, hs)], s_w).start()

    def send(src, dst, ssem, rsem, pipe, seq):
        pltpu.make_async_remote_copy(
            src_ref=src, dst_ref=dst, send_sem=ssem, recv_sem=rsem,
            device_id=(pipe, seq), device_id_type=MESH,
        ).start()

    def local(src, dst, sem):
        pltpu.make_async_copy(src, dst, sem).start()

    def await_bytes(region, sem):
        pltpu.make_async_copy(region, region, sem).wait()

    def other(k):
        return lax.rem(h + k, count)

    barrier = pltpu.get_barrier_semaphore()
    for k in range(1, SIDE * SIDE):
        pl.semaphore_signal(barrier, inc=1, device_id=(l, other(k)), device_id_type=MESH)
    for k in range(SIDE):
        pl.semaphore_signal(barrier, inc=1, device_id=(nxt, SIDE * i + k), device_id_type=MESH)
        pl.semaphore_signal(barrier, inc=1, device_id=(prv, SIDE * i + k), device_id_type=MESH)

    @pl.when(l == 0)
    def _():
        for p in range(2):
            for q in range(SIDE):
                local(hid.at[p, :, pl.ds(q * piece, piece)], xp.at[p, q], r_xp.at[p])

    pl.semaphore_wait(barrier, SIDE * SIDE - 1 + 2 * SIDE)

    def send_out_proj():
        for k in range(1, SIDE * SIDE):
            t = other(k)
            col = pl.multiple_of(lax.rem(t, SIDE) * piece, 128)
            send(o.at[:, pl.ds(col, piece)], og.at[h], s_o, r_o, l, t)
        col = pl.multiple_of(j * piece, 128)
        local(o.at[:, pl.ds(col, piece)], og.at[h], r_o)

    def send_rows():
        for k in range(1, SIDE):
            jj = lax.rem(j + k, SIDE)
            col = pl.multiple_of(jj * piece, 128)
            send(o.at[:, pl.ds(col, piece)], og.at[j], s_o, r_o, l, SIDE * i + jj)
        col = pl.multiple_of(j * piece, 128)
        local(o.at[:, pl.ds(col, piece)], og.at[j], r_o)

    def send_stale():
        for k in range(1, SIDE * SIDE):
            t = other(k)
            send(st.at[t], sg.at[h], s_st, r_st, l, t)
        local(st.at[h], sg.at[h], r_st)

    send_stale()

    @pl.when(~early)
    def _():
        send_out_proj()

    @pl.when(l == 1)
    def _():
        pl.semaphore_wait(go, 1)
        send_rows()

    def start(p):
        await_bytes(xp.at[p], r_xp.at[p])
        x = xp[p].astype(jnp.float32)
        width = SIDE * piece
        mean = jnp.sum(jnp.sum(x, axis=0), axis=-1, keepdims=True) / width
        cen = x - mean[None]
        spread = jnp.sum(jnp.sum(cen * cen, axis=0), axis=-1, keepdims=True) / width
        inv = 1.0 / jnp.sqrt(spread + 1e-06)
        normed = (cen * inv[None] * (1.0 + scale[...]) + shift[...]).astype(jnp.bfloat16)
        nga[p, i, j, :, :piece] = normed[0]
        nga[p, i, j, :, piece:] = normed[1]
        ngb[p, j, i, :, :piece] = normed[2]
        ngb[p, j, i, :, piece:] = normed[3]

    def own_blocks(p):
        for k in (1, 3, 2):
            jj = lax.rem(j + k, SIDE)
            ii = lax.rem(i + k, SIDE)
            send(nga.at[p, i, j], nga.at[p, i, j], s_1a.at[p], r_1a.at[p, j], l, SIDE * i + jj)
            send(ngb.at[p, j, i], ngb.at[p, j, i], s_1b.at[p], r_1b.at[p, i], l, SIDE * ii + j)

        forward(p, i, j)

    def forward(p, isrc, jsrc):
        for k in (1, 3, 2):
            jj = lax.rem(j + k, SIDE)
            ii = lax.rem(i + k, SIDE)
            send(nga.at[p, i, jsrc], nga.at[p, i, jsrc], s_2a.at[p], r_2a.at[p, i], l, SIDE * ii + j)
            send(ngb.at[p, j, isrc], ngb.at[p, j, isrc], s_2b.at[p], r_2b.at[p, j], l, SIDE * i + jj)

    def relay(p):
        for k in (1, 3, 2):
            jj = lax.rem(j + k, SIDE)
            ii = lax.rem(i + k, SIDE)
            await_bytes(nga.at[p, i, jj], r_1a.at[p, jj])
            await_bytes(ngb.at[p, j, ii], r_1b.at[p, ii])
            forward(p, ii, jj)
        for k in range(1, SIDE):
            jj = lax.rem(j + k, SIDE)
            send(xp.at[p, jj], xr.at[p, j], s_xr.at[p], r_xr.at[p], l, SIDE * i + jj)
        local(xp.at[p, j], xr.at[p, j], r_xr.at[p])


    def settle():
        @pl.when(l == 0)
        def _():
            send_rows()

        await_bytes(w, s_w)
        await_bytes(sg, r_st)
        for c in range(2):
            old = sg[:, c].astype(jnp.float32).reshape(count * rows, hs)
            kv[0, c] = old.astype(jnp.bfloat16)

    def project(p):
        def arrive(step, c):
            k = step + lax.div(step, 2) * (5 - 2 * step)
            ii = lax.rem(i + k, SIDE)
            jj = lax.rem(j + k, SIDE)

            @pl.when(step > 0)
            def _():
                await_bytes(nga.at[p, ii], r_2a.at[p, ii])

            left = jnp.concatenate([nga[p, ii, m].astype(jnp.float32) for m in range(SIDE)], axis=0)
            pa[ii] = jnp.dot(
                left.astype(jnp.bfloat16), w[:half], preferred_element_type=jnp.float32
            )

            @pl.when(step > 0)
            def _():
                await_bytes(ngb.at[p, jj], r_2b.at[p, jj])

            right = jnp.concatenate([ngb[p, jj, m].astype(jnp.float32) for m in range(SIDE)], axis=0)
            right = jnp.dot(
                right.astype(jnp.bfloat16), w[half:], preferred_element_type=jnp.float32
            )
            pb[jj] = right.reshape(SIDE, rows, 3 * hs)
            return c

        lax.fori_loop(0, SIDE, arrive, 0, unroll=True)

        def heads(g, c):
            out = pa[g] + pb[:, g].reshape(group, 3 * hs)
            for c in range(2):
                part = out[:, c * hs : (c + 1) * hs]
                square = jnp.mean(part * part, axis=-1, keepdims=True)
                part = part * (1.0 / jnp.sqrt(square + 1e-06)) * gain[c : c + 1, :]
                if c == 0:
                    qb[g] = part.astype(jnp.bfloat16)
                else:
                    keys = part
            values = out[:, 2 * hs :]
            kv[p + 1, 0, pl.ds(pl.multiple_of(g * group, group), group)] = keys.astype(jnp.bfloat16)
            kv[p + 1, 1, pl.ds(pl.multiple_of(g * group, group), group)] = values.astype(jnp.bfloat16)
            fcs[p, pl.ds(g * SIDE, SIDE), 0] = keys.reshape(SIDE, rows, hs).astype(jnp.bfloat16)
            fcs[p, pl.ds(g * SIDE, SIDE), 1] = values.reshape(SIDE, rows, hs).astype(jnp.bfloat16)
            return c

        lax.fori_loop(0, SIDE, heads, 0, unroll=True)

    def attend(p):
        def one(g):
            q = qb[g]
            dims = (((1,), (1,)), ((), ()))
            near = lax.dot_general(q, kv[p + 1, 0], dims, preferred_element_type=jnp.float32)
            far = lax.dot_general(q, kv[p, 0], dims, preferred_element_type=jnp.float32)
            near = jnp.exp(near * factor)
            far = jnp.exp(far * factor)
            den = jnp.sum(near, axis=-1, keepdims=True) + jnp.sum(far, axis=-1, keepdims=True)
            inv = 1.0 / den
            near = (near * inv).astype(jnp.bfloat16)
            far = (far * inv).astype(jnp.bfloat16)
            mixed = jnp.dot(near, kv[p + 1, 1], preferred_element_type=jnp.float32)
            mixed = mixed + jnp.dot(far, kv[p, 1], preferred_element_type=jnp.float32)
            att[p, g] = mixed.astype(jnp.bfloat16)

        for gg in (2, 1, 3, 0):
            g = lax.rem(i + gg, SIDE)
            one(g)

            @pl.when(early)
            def _():
                for k in range(1, SIDE):
                    jj = lax.rem(j + k, SIDE)
                    send(att.at[p, g], atg.at[p, SIDE * j + g], s_at.at[p], r_at.at[p], l, SIDE * i + jj)
                local(att.at[p, g], atg.at[p, SIDE * j + g], r_at.at[p])

            @pl.when(~early)
            def _():
                for k in range(1 if gg == 0 else 0, SIDE):
                    jj = lax.rem(j + k, SIDE)
                    send(att.at[p, g], atg.at[p, h], s_at.at[p], r_at.at[p], l, SIDE * g + jj)
                if gg == 0:
                    local(att.at[p, g], atg.at[p, h], r_at.at[p])

    def by_heads(p):
        if p == 0:
            await_bytes(og.at[pl.ds(0, SIDE)], r_o)
        weight = og[0:SIDE].reshape(SIDE * hs, piece)
        await_bytes(atg.at[p], r_at.at[p])
        for gg in (2, 1, 3, 0):
            g = lax.rem(i + gg, SIDE)
            mixed = jnp.concatenate([atg[p, SIDE * m + g] for m in range(SIDE)], axis=1)
            part = jnp.dot(mixed, weight, preferred_element_type=jnp.float32)
            if gg == 0:
                up[...] = part
            else:
                prs[p, g] = part.astype(jnp.bfloat16)
                send(prs.at[p, g], rs.at[p, i], s_rs.at[p], r_rs.at[p], l, SIDE * g + j)
        await_bytes(rs.at[p, pl.ds(0, SIDE - 1)], r_rs.at[p])
        total = up[...]
        for gg in range(1, SIDE):
            total = total + rs[p, lax.rem(i + gg, SIDE)].astype(jnp.float32)
        up[...] = total

    def by_tokens(p):
        if p == 0:
            await_bytes(og, r_o)
        await_bytes(atg.at[p], r_at.at[p])
        mixed = jnp.concatenate([atg[p, m] for m in range(SIDE * SIDE)], axis=1)
        up[...] = jnp.dot(
            mixed, og[...].reshape(SIDE * SIDE * hs, piece), preferred_element_type=jnp.float32
        )

    def finish(p):
        await_bytes(xr.at[p], r_xr.at[p])

        @pl.when(early)
        def _():
            by_heads(p)

        @pl.when(~early)
        def _():
            by_tokens(p)

        base = xr[p].astype(jnp.float32).reshape(group, piece)
        result = base + gate[j] * up[...]
        xo[p] = result.reshape(SIDE, rows, piece).astype(jnp.bfloat16)

        @pl.when(l < sections - 1)
        def _():
            for k in range(SIDE):
                send(xo.at[p, k], xp.at[p, j], s_xp.at[p], r_xp.at[p], nxt, SIDE * i + k)

        for k in range(1, SIDE):
            kk = lax.rem(j + k, SIDE)
            send(xo.at[p, kk], bob.at[p, j], s_bo.at[p], r_bo.at[p], l, SIDE * i + kk)
        local(xo.at[p, j], bob.at[p, j], r_bo.at[p])

    def send_cache(p):
        for k in range(1, SIDE * SIDE):
            t = other(k)
            send(fcs.at[p, t], fcb.at[p, h], s_fc.at[p], r_fc.at[p], l, t)
        local(fcs.at[p, h], fcb.at[p, h], r_fc.at[p])

    start(0)
    own_blocks(0)
    relay(0)
    settle()

    @pl.when(odd)
    def _():
        pl.semaphore_signal(go, inc=1, device_id=(prv, h), device_id_type=MESH)

    project(0)

    attend(0)
    finish(0)

    @pl.when(l == 0)
    def _():
        pl.semaphore_signal(go, inc=1, device_id=(nxt, h), device_id_type=MESH)

    start(1)

    @pl.when(~odd)
    def _():
        pl.semaphore_wait(go, 1)

    own_blocks(1)
    relay(1)
    project(1)
    attend(1)
    send_cache(0)
    finish(1)
    send_cache(1)

    for p in range(2):
        await_bytes(fcb.at[p], r_fc.at[p])
        await_bytes(bob.at[p], r_bo.at[p])
    fc_out[...] = fcb[...]
    for p in range(2):
        for q in range(SIDE):
            bo_out[p, :, q * piece : (q + 1) * piece] = bob[p, q].astype(jnp.float32)
    most = pl.ds(0, SIDE * SIDE - 1)
    three = pl.ds(0, SIDE - 1)
    await_bytes(sg.at[most], s_st)
    for p in range(2):
        await_bytes(nga.at[p, 0, three], s_1a.at[p])
        await_bytes(ngb.at[p, 0, three], s_1b.at[p])
        await_bytes(nga.at[p, three], s_2a.at[p])
        await_bytes(ngb.at[p, three], s_2b.at[p])
        await_bytes(xr.at[p, three], s_xr.at[p])
        await_bytes(fcb.at[p, most], s_fc.at[p])
        await_bytes(bob.at[p, three], s_bo.at[p])

    @pl.when(early)
    def _():
        await_bytes(og.at[three], s_o)
        for p in range(2):
            await_bytes(atg.at[p, pl.ds(0, SIDE * (SIDE - 1))], s_at.at[p])
            await_bytes(rs.at[p, three], s_rs.at[p])

    @pl.when(~early)
    def _():
        await_bytes(og.at[most], s_o)
        for p in range(2):
            await_bytes(atg.at[p, most], s_at.at[p])

    @pl.when(l < sections - 1)
    def _():
        for p in range(2):
            await_bytes(xp.at[p], s_xp.at[p])


def body(hidden, mod_shift, mod_scale, mod_gate, norm_gain, input_proj, output_proj, stale_cache):
    patches, rows, width = hidden.shape
    hs = norm_gain.shape[2]
    count = SIDE * SIDE
    piece = width // SIDE
    half = width // 2
    bf, f32 = jnp.bfloat16, jnp.float32
    shift = mod_shift.reshape(SIDE, 1, piece)
    scale = mod_scale.reshape(SIDE, 1, piece)
    gate = mod_gate.reshape(SIDE, 1, piece)
    w = input_proj[0].transpose(1, 0, 2)
    st = stale_cache[0, 1].reshape(rows, 2, count, hs).transpose(2, 1, 0, 3)
    vmem = pl.BlockSpec(memory_space=pltpu.VMEM)
    hbm = pl.BlockSpec(memory_space=pl.ANY)
    one = pltpu.SemaphoreType.DMA
    pair = pltpu.SemaphoreType.DMA((2,))
    quad = pltpu.SemaphoreType.DMA((2, SIDE))
    bo, fc = pl.pallas_call(
        block_kernel,
        out_shape=(
            jax.ShapeDtypeStruct((patches, rows, width), f32),
            jax.ShapeDtypeStruct((patches, count, 2, rows, hs), bf),
        ),
        in_specs=[vmem] * 5 + [hbm, hbm, vmem],
        out_specs=(vmem, vmem),
        scratch_shapes=[
            pltpu.VMEM((patches, SIDE, rows, piece), bf),
            pltpu.VMEM((patches, SIDE, SIDE, rows, half), bf),
            pltpu.VMEM((patches, SIDE, SIDE, rows, half), bf),
            pltpu.VMEM((patches, SIDE, rows, piece), bf),
            pltpu.VMEM((count, 2, rows, hs), bf),
            pltpu.VMEM((patches + 1, 2, count * rows, hs), bf),
            pltpu.VMEM((SIDE, SIDE * rows, hs), bf),
            pltpu.VMEM((count, hs, piece), bf),
            pltpu.VMEM((patches, SIDE, SIDE * rows, hs), bf),
            pltpu.VMEM((patches, count, SIDE * rows, hs), bf),
            pltpu.VMEM((patches, SIDE, rows, piece), bf),
            pltpu.VMEM((patches, SIDE, rows, piece), bf),
            pltpu.VMEM((patches, count, 2, rows, hs), bf),
            pltpu.VMEM((patches, count, 2, rows, hs), bf),
            one, one, one, one,
        ] + [pair] * 4 + [pair, quad] * 4 + [pair] * 6 + [
            pltpu.VMEM((width, 3 * hs), bf),
            one,
            pltpu.SemaphoreType.REGULAR,
            pltpu.VMEM((SIDE, SIDE * rows, 3 * hs), f32),
            pltpu.VMEM((SIDE, SIDE, rows, 3 * hs), f32),
            pltpu.VMEM((SIDE * rows, piece), f32),
            pltpu.VMEM((patches, SIDE, SIDE * rows, piece), bf),
            pltpu.VMEM((patches, SIDE, SIDE * rows, piece), bf),
            pair, pair,
        ],
        compiler_params=pltpu.CompilerParams(
            collective_id=0, has_side_effects=True, vmem_limit_bytes=56 * 1024 * 1024
        ),
    )(hidden, shift, scale, gate, norm_gain[0], w, output_proj[0], st)
    outputs = bo.astype(bf)[None]
    cache = fc.transpose(0, 3, 2, 1, 4).reshape(1, patches, rows, 2, count * hs)
    return outputs, cache


def solution(mesh):
    in_specs = (
        P(None, "seq", None),
        P("pipe", None),
        P("pipe", None),
        P("pipe", None),
        P("pipe", None, None),
        P("pipe", None, None, "seq"),
        P("pipe", "seq", None),
        P("pipe", None, "seq", None, None),
    )
    out_specs = (P("pipe", None, "seq", None), P("pipe", None, "seq", None, None))
    return jax.shard_map(body, mesh=mesh, in_specs=in_specs, out_specs=out_specs, check_vma=False)
```

```python
import functools
import math

import jax
import jax.numpy as jnp
from jax import lax
from jax.experimental import pallas as pl
from jax.experimental.pallas import tpu as pltpu
from jax.sharding import PartitionSpec as P

MESH = pl.DeviceIdType.MESH
SIDE = 4


def block_kernel(
    hid, shift, scale, gate, gain, w_hbm, o, st, bo_out, fc_out,
    xp, nga, ngb, xr, sg, kv, qb, og, att, atg, xo, bob, fcs, fcb,
    s_st, r_st, s_o, r_o, s_xp, r_xp, s_xr, r_xr, s_1a, r_1a, s_1b, r_1b,
    s_2a, r_2a, s_2b, r_2b, s_at, r_at, s_fc, r_fc, s_bo, r_bo, w, s_w, go, pa, pb,
    up, prs, rs, s_rs, r_rs,
):
    l = lax.axis_index("pipe")
    h = lax.axis_index("seq")
    sections = lax.axis_size("pipe")
    count = lax.axis_size("seq")
    i = lax.div(h, SIDE)
    j = lax.rem(h, SIDE)
    half = w.shape[0] // 2
    rows, piece = xp.shape[2], xp.shape[3]
    group = SIDE * rows
    hs = gain.shape[1]
    factor = 1.0 / math.sqrt(hs)
    nxt = lax.rem(l + 1, sections)
    prv = lax.rem(l + sections - 1, sections)
    odd = lax.rem(l, 2) == 1
    early = l < 2
    for m in range(3):
        pltpu.make_async_copy(w_hbm.at[m], w.at[:, pl.ds(m * hs, hs)], s_w).start()

    def send(src, dst, ssem, rsem, pipe, seq):
        pltpu.make_async_remote_copy(
            src_ref=src, dst_ref=dst, send_sem=ssem, recv_sem=rsem,
            device_id=(pipe, seq), device_id_type=MESH,
        ).start()

    def local(src, dst, sem):
        pltpu.make_async_copy(src, dst, sem).start()

    def await_bytes(region, sem):
        pltpu.make_async_copy(region, region, sem).wait()

    def other(k):
        return lax.rem(h + k, count)

    barrier = pltpu.get_barrier_semaphore()
    for k in range(1, SIDE * SIDE):
        pl.semaphore_signal(barrier, inc=1, device_id=(l, other(k)), device_id_type=MESH)
    for k in range(SIDE):
        pl.semaphore_signal(barrier, inc=1, device_id=(nxt, SIDE * i + k), device_id_type=MESH)
        pl.semaphore_signal(barrier, inc=1, device_id=(prv, SIDE * i + k), device_id_type=MESH)

    @pl.when(l == 0)
    def _():
        for p in range(2):
            for q in range(SIDE):
                local(hid.at[p, :, pl.ds(q * piece, piece)], xp.at[p, q], r_xp.at[p])

    pl.semaphore_wait(barrier, SIDE * SIDE - 1 + 2 * SIDE)

    def send_out_proj():
        for k in range(1, SIDE * SIDE):
            t = other(k)
            col = pl.multiple_of(lax.rem(t, SIDE) * piece, 128)
            send(o.at[:, pl.ds(col, piece)], og.at[h], s_o, r_o, l, t)
        col = pl.multiple_of(j * piece, 128)
        local(o.at[:, pl.ds(col, piece)], og.at[h], r_o)

    def send_rows():
        for k in range(1, SIDE):
            jj = lax.rem(j + k, SIDE)
            col = pl.multiple_of(jj * piece, 128)
            send(o.at[:, pl.ds(col, piece)], og.at[j], s_o, r_o, l, SIDE * i + jj)
        col = pl.multiple_of(j * piece, 128)
        local(o.at[:, pl.ds(col, piece)], og.at[j], r_o)

    def send_stale():
        for k in range(1, SIDE * SIDE):
            t = other(k)
            send(st.at[t], sg.at[h], s_st, r_st, l, t)
        local(st.at[h], sg.at[h], r_st)

    send_stale()

    @pl.when(~early)
    def _():
        send_out_proj()

    @pl.when(l == 1)
    def _():
        pl.semaphore_wait(go, 1)
        send_rows()

    def start(p):
        await_bytes(xp.at[p], r_xp.at[p])
        x = xp[p].astype(jnp.float32)
        width = SIDE * piece
        mean = jnp.sum(jnp.sum(x, axis=0), axis=-1, keepdims=True) / width
        cen = x - mean[None]
        spread = jnp.sum(jnp.sum(cen * cen, axis=0), axis=-1, keepdims=True) / width
        inv = 1.0 / jnp.sqrt(spread + 1e-06)
        normed = (cen * inv[None] * (1.0 + scale[...]) + shift[...]).astype(jnp.bfloat16)
        nga[p, i, j, :, :piece] = normed[0]
        nga[p, i, j, :, piece:] = normed[1]
        ngb[p, j, i, :, :piece] = normed[2]
        ngb[p, j, i, :, piece:] = normed[3]

    def own_blocks(p):
        for k in (1, 3, 2):
            jj = lax.rem(j + k, SIDE)
            ii = lax.rem(i + k, SIDE)
            send(nga.at[p, i, j], nga.at[p, i, j], s_1a.at[p], r_1a.at[p, j], l, SIDE * i + jj)
            send(ngb.at[p, j, i], ngb.at[p, j, i], s_1b.at[p], r_1b.at[p, i], l, SIDE * ii + j)

        forward(p, i, j)

    def forward(p, isrc, jsrc):
        for k in (1, 3, 2):
            jj = lax.rem(j + k, SIDE)
            ii = lax.rem(i + k, SIDE)
            send(nga.at[p, i, jsrc], nga.at[p, i, jsrc], s_2a.at[p], r_2a.at[p, i], l, SIDE * ii + j)
            send(ngb.at[p, j, isrc], ngb.at[p, j, isrc], s_2b.at[p], r_2b.at[p, j], l, SIDE * i + jj)

    def relay(p):
        for k in (1, 3, 2):
            jj = lax.rem(j + k, SIDE)
            ii = lax.rem(i + k, SIDE)
            await_bytes(nga.at[p, i, jj], r_1a.at[p, jj])
            await_bytes(ngb.at[p, j, ii], r_1b.at[p, ii])
            forward(p, ii, jj)
        for k in range(1, SIDE):
            jj = lax.rem(j + k, SIDE)
            send(xp.at[p, jj], xr.at[p, j], s_xr.at[p], r_xr.at[p], l, SIDE * i + jj)
        local(xp.at[p, j], xr.at[p, j], r_xr.at[p])


    def settle():
        @pl.when(l == 0)
        def _():
            send_rows()

        await_bytes(w, s_w)
        await_bytes(sg, r_st)
        for c in range(2):
            old = sg[:, c].astype(jnp.float32).reshape(count * rows, hs)
            kv[c, 0] = old.astype(jnp.bfloat16)

    def project(p):
        def arrive(step, c):
            k = step + lax.div(step, 2) * (5 - 2 * step)
            ii = lax.rem(i + k, SIDE)
            jj = lax.rem(j + k, SIDE)

            @pl.when(step > 0)
            def _():
                await_bytes(nga.at[p, ii], r_2a.at[p, ii])

            left = jnp.concatenate([nga[p, ii, m].astype(jnp.float32) for m in range(SIDE)], axis=0)
            pa[ii] = jnp.dot(
                left.astype(jnp.bfloat16), w[:half], preferred_element_type=jnp.float32
            )

            @pl.when(step > 0)
            def _():
                await_bytes(ngb.at[p, jj], r_2b.at[p, jj])

            right = jnp.concatenate([ngb[p, jj, m].astype(jnp.float32) for m in range(SIDE)], axis=0)
            right = jnp.dot(
                right.astype(jnp.bfloat16), w[half:], preferred_element_type=jnp.float32
            )
            pb[jj] = right.reshape(SIDE, rows, 3 * hs)
            return c

        lax.fori_loop(0, SIDE, arrive, 0, unroll=True)

        def heads(g, c):
            out = pa[g] + pb[:, g].reshape(group, 3 * hs)
            for c in range(2):
                part = out[:, c * hs : (c + 1) * hs]
                square = jnp.mean(part * part, axis=-1, keepdims=True)
                part = part * (1.0 / jnp.sqrt(square + 1e-06)) * gain[c : c + 1, :]
                if c == 0:
                    qb[g] = part.astype(jnp.bfloat16)
                else:
                    keys = part
            values = out[:, 2 * hs :]
            kv[0, p + 1, pl.ds(pl.multiple_of(g * group, group), group)] = keys.astype(jnp.bfloat16)
            kv[1, p + 1, pl.ds(pl.multiple_of(g * group, group), group)] = values.astype(jnp.bfloat16)
            fcs[p, pl.ds(g * SIDE, SIDE), 0] = keys.reshape(SIDE, rows, hs).astype(jnp.bfloat16)
            fcs[p, pl.ds(g * SIDE, SIDE), 1] = values.reshape(SIDE, rows, hs).astype(jnp.bfloat16)
            return c

        lax.fori_loop(0, SIDE, heads, 0, unroll=True)

    def attend(p):
        def one(g):
            q = qb[g]
            dims = (((1,), (1,)), ((), ()))
            keys = kv[0, p : p + 2].reshape(2 * count * rows, hs)
            values = kv[1, p : p + 2].reshape(2 * count * rows, hs)
            weights = lax.dot_general(q, keys, dims, preferred_element_type=jnp.float32)
            weights = jnp.exp(weights * factor)
            inv = 1.0 / jnp.sum(weights, axis=-1, keepdims=True)
            probs = (weights * inv).astype(jnp.bfloat16)
            mixed = jnp.dot(probs, values, preferred_element_type=jnp.float32)
            att[p, g] = mixed.astype(jnp.bfloat16)

        for gg in (2, 1, 3, 0):
            g = lax.rem(i + gg, SIDE)
            one(g)

            @pl.when(early)
            def _():
                for k in range(1, SIDE):
                    jj = lax.rem(j + k, SIDE)
                    send(att.at[p, g], atg.at[p, SIDE * j + g], s_at.at[p], r_at.at[p], l, SIDE * i + jj)
                local(att.at[p, g], atg.at[p, SIDE * j + g], r_at.at[p])

            @pl.when(~early)
            def _():
                for k in range(1 if gg == 0 else 0, SIDE):
                    jj = lax.rem(j + k, SIDE)
                    send(att.at[p, g], atg.at[p, h], s_at.at[p], r_at.at[p], l, SIDE * g + jj)
                if gg == 0:
                    local(att.at[p, g], atg.at[p, h], r_at.at[p])

    def add_up(p, update):
        base = xr[p].astype(jnp.float32).reshape(group, piece)
        result = base + gate[j] * update
        xo[p] = result.reshape(SIDE, rows, piece).astype(jnp.bfloat16)

    def by_heads(p):
        if p == 0:
            await_bytes(og.at[pl.ds(0, SIDE)], r_o)
        weight = og[0:SIDE].reshape(SIDE * hs, piece)
        await_bytes(atg.at[p], r_at.at[p])
        for gg in (2, 1, 3, 0):
            g = lax.rem(i + gg, SIDE)
            mixed = jnp.concatenate([atg[p, SIDE * m + g] for m in range(SIDE)], axis=1)
            part = jnp.dot(mixed, weight, preferred_element_type=jnp.float32)
            if gg == 0:
                up[...] = part
            else:
                prs[p, g] = part.astype(jnp.bfloat16)
                send(prs.at[p, g], rs.at[p, i], s_rs.at[p], r_rs.at[p], l, SIDE * g + j)
        await_bytes(rs.at[p, pl.ds(0, SIDE - 1)], r_rs.at[p])
        total = up[...]
        for gg in range(1, SIDE):
            total = total + rs[p, lax.rem(i + gg, SIDE)].astype(jnp.float32)
        add_up(p, total)

    def by_tokens(p):
        if p == 0:
            await_bytes(og, r_o)
        await_bytes(atg.at[p], r_at.at[p])
        mixed = jnp.concatenate([atg[p, m] for m in range(SIDE * SIDE)], axis=1)
        weight = og[...].reshape(SIDE * SIDE * hs, piece)
        update = jnp.dot(mixed, weight, preferred_element_type=jnp.float32)
        add_up(p, update)

    def finish(p):
        await_bytes(xr.at[p], r_xr.at[p])

        @pl.when(early)
        def _():
            by_heads(p)

        @pl.when(~early)
        def _():
            by_tokens(p)

        @pl.when(l < sections - 1)
        def _():
            for k in range(SIDE):
                send(xo.at[p, k], xp.at[p, j], s_xp.at[p], r_xp.at[p], nxt, SIDE * i + k)

        for k in range(1, SIDE):
            kk = lax.rem(j + k, SIDE)
            send(xo.at[p, kk], bob.at[p, j], s_bo.at[p], r_bo.at[p], l, SIDE * i + kk)
        local(xo.at[p, j], bob.at[p, j], r_bo.at[p])

    def send_cache(p):
        for k in range(1, SIDE * SIDE):
            t = other(k)
            send(fcs.at[p, t], fcb.at[p, h], s_fc.at[p], r_fc.at[p], l, t)
        local(fcs.at[p, h], fcb.at[p, h], r_fc.at[p])

    start(0)
    own_blocks(0)
    relay(0)
    settle()

    @pl.when(odd)
    def _():
        pl.semaphore_signal(go, inc=1, device_id=(prv, h), device_id_type=MESH)

    project(0)

    attend(0)
    finish(0)

    @pl.when(l == 0)
    def _():
        pl.semaphore_signal(go, inc=1, device_id=(nxt, h), device_id_type=MESH)

    start(1)

    @pl.when(~odd)
    def _():
        pl.semaphore_wait(go, 1)

    own_blocks(1)
    relay(1)
    project(1)
    attend(1)
    send_cache(0)
    send_cache(1)
    finish(1)

    for p in range(2):
        await_bytes(fcb.at[p], r_fc.at[p])
        await_bytes(bob.at[p], r_bo.at[p])
    fc_out[...] = fcb[...]
    for p in range(2):
        for q in range(SIDE):
            bo_out[p, :, q * piece : (q + 1) * piece] = bob[p, q].astype(jnp.float32)
    most = pl.ds(0, SIDE * SIDE - 1)
    three = pl.ds(0, SIDE - 1)
    await_bytes(sg.at[most], s_st)
    for p in range(2):
        await_bytes(nga.at[p, 0, three], s_1a.at[p])
        await_bytes(ngb.at[p, 0, three], s_1b.at[p])
        await_bytes(nga.at[p, three], s_2a.at[p])
        await_bytes(ngb.at[p, three], s_2b.at[p])
        await_bytes(xr.at[p, three], s_xr.at[p])
        await_bytes(fcb.at[p, most], s_fc.at[p])
        await_bytes(bob.at[p, three], s_bo.at[p])

    @pl.when(early)
    def _():
        await_bytes(og.at[three], s_o)
        for p in range(2):
            await_bytes(atg.at[p, pl.ds(0, SIDE * (SIDE - 1))], s_at.at[p])
            await_bytes(rs.at[p, three], s_rs.at[p])

    @pl.when(~early)
    def _():
        await_bytes(og.at[most], s_o)
        for p in range(2):
            await_bytes(atg.at[p, most], s_at.at[p])

    @pl.when(l < sections - 1)
    def _():
        for p in range(2):
            await_bytes(xp.at[p], s_xp.at[p])


def body(hidden, mod_shift, mod_scale, mod_gate, norm_gain, input_proj, output_proj, stale_cache):
    patches, rows, width = hidden.shape
    hs = norm_gain.shape[2]
    count = SIDE * SIDE
    piece = width // SIDE
    half = width // 2
    bf, f32 = jnp.bfloat16, jnp.float32
    shift = mod_shift.reshape(SIDE, 1, piece)
    scale = mod_scale.reshape(SIDE, 1, piece)
    gate = mod_gate.reshape(SIDE, 1, piece)
    w = input_proj[0].transpose(1, 0, 2)
    st = stale_cache[0, 1].reshape(rows, 2, count, hs).transpose(2, 1, 0, 3)
    vmem = pl.BlockSpec(memory_space=pltpu.VMEM)
    hbm = pl.BlockSpec(memory_space=pl.ANY)
    one = pltpu.SemaphoreType.DMA
    pair = pltpu.SemaphoreType.DMA((2,))
    quad = pltpu.SemaphoreType.DMA((2, SIDE))
    bo, fc = pl.pallas_call(
        block_kernel,
        out_shape=(
            jax.ShapeDtypeStruct((patches, rows, width), f32),
            jax.ShapeDtypeStruct((patches, count, 2, rows, hs), bf),
        ),
        in_specs=[vmem] * 5 + [hbm, hbm, vmem],
        out_specs=(vmem, vmem),
        scratch_shapes=[
            pltpu.VMEM((patches, SIDE, rows, piece), bf),
            pltpu.VMEM((patches, SIDE, SIDE, rows, half), bf),
            pltpu.VMEM((patches, SIDE, SIDE, rows, half), bf),
            pltpu.VMEM((patches, SIDE, rows, piece), bf),
            pltpu.VMEM((count, 2, rows, hs), bf),
            pltpu.VMEM((2, patches + 1, count * rows, hs), bf),
            pltpu.VMEM((SIDE, SIDE * rows, hs), bf),
            pltpu.VMEM((count, hs, piece), bf),
            pltpu.VMEM((patches, SIDE, SIDE * rows, hs), bf),
            pltpu.VMEM((patches, count, SIDE * rows, hs), bf),
            pltpu.VMEM((patches, SIDE, rows, piece), bf),
            pltpu.VMEM((patches, SIDE, rows, piece), bf),
            pltpu.VMEM((patches, count, 2, rows, hs), bf),
            pltpu.VMEM((patches, count, 2, rows, hs), bf),
            one, one, one, one,
        ] + [pair] * 4 + [pair, quad] * 4 + [pair] * 6 + [
            pltpu.VMEM((width, 3 * hs), bf),
            one,
            pltpu.SemaphoreType.REGULAR,
            pltpu.VMEM((SIDE, SIDE * rows, 3 * hs), f32),
            pltpu.VMEM((SIDE, SIDE, rows, 3 * hs), f32),
            pltpu.VMEM((SIDE * rows, piece), f32),
            pltpu.VMEM((patches, SIDE, SIDE * rows, piece), bf),
            pltpu.VMEM((patches, SIDE, SIDE * rows, piece), bf),
            pair, pair,
        ],
        compiler_params=pltpu.CompilerParams(
            collective_id=0, has_side_effects=True, vmem_limit_bytes=56 * 1024 * 1024
        ),
    )(hidden, shift, scale, gate, norm_gain[0], w, output_proj[0], st)
    outputs = bo.astype(bf)[None]
    cache = fc.transpose(0, 3, 2, 1, 4).reshape(1, patches, rows, 2, count * hs)
    return outputs, cache


def solution(mesh):
    in_specs = (
        P(None, "seq", None),
        P("pipe", None),
        P("pipe", None),
        P("pipe", None),
        P("pipe", None, None),
        P("pipe", None, None, "seq"),
        P("pipe", "seq", None),
        P("pipe", None, "seq", None, None),
    )
    out_specs = (P("pipe", None, "seq", None), P("pipe", None, "seq", None, None))
    return jax.shard_map(body, mesh=mesh, in_specs=in_specs, out_specs=out_specs, check_vma=False)
```

```python
import functools
import math

import jax
import jax.numpy as jnp
from jax import lax
from jax.experimental import pallas as pl
from jax.experimental.pallas import tpu as pltpu
from jax.sharding import PartitionSpec as P

MESH = pl.DeviceIdType.MESH
SIDE = 4


def block_kernel(
    hid, shift, scale, gate, gain, w_hbm, o, st, bo_out, fc_out,
    xp, nga, ngb, xr, sg, kv, qb, og, att, atg, xo, bob, fcs, fcb,
    s_st, r_st, s_o, r_o, s_xp, r_xp, s_xr, r_xr, s_1a, r_1a, s_1b, r_1b,
    s_2a, r_2a, s_2b, r_2b, s_at, r_at, s_fc, r_fc, s_bo, r_bo, w, s_w, go, pa, pb,
    up, prs, rs, s_rs, r_rs,
):
    l = lax.axis_index("pipe")
    h = lax.axis_index("seq")
    sections = lax.axis_size("pipe")
    count = lax.axis_size("seq")
    i = lax.div(h, SIDE)
    j = lax.rem(h, SIDE)
    half = w.shape[0] // 2
    rows, piece = xp.shape[2], xp.shape[3]
    group = SIDE * rows
    hs = gain.shape[1]
    factor = 1.0 / math.sqrt(hs)
    nxt = lax.rem(l + 1, sections)
    prv = lax.rem(l + sections - 1, sections)
    odd = lax.rem(l, 2) == 1
    early = l < 2
    for m in range(3):
        pltpu.make_async_copy(w_hbm.at[m], w.at[:, pl.ds(m * hs, hs)], s_w).start()

    def send(src, dst, ssem, rsem, pipe, seq):
        pltpu.make_async_remote_copy(
            src_ref=src, dst_ref=dst, send_sem=ssem, recv_sem=rsem,
            device_id=(pipe, seq), device_id_type=MESH,
        ).start()

    def local(src, dst, sem):
        pltpu.make_async_copy(src, dst, sem).start()

    def await_bytes(region, sem):
        pltpu.make_async_copy(region, region, sem).wait()

    def other(k):
        return lax.rem(h + k, count)

    barrier = pltpu.get_barrier_semaphore()
    for k in range(1, SIDE * SIDE):
        pl.semaphore_signal(barrier, inc=1, device_id=(l, other(k)), device_id_type=MESH)
    for k in range(SIDE):
        pl.semaphore_signal(barrier, inc=1, device_id=(nxt, SIDE * i + k), device_id_type=MESH)
        pl.semaphore_signal(barrier, inc=1, device_id=(prv, SIDE * i + k), device_id_type=MESH)

    @pl.when(l == 0)
    def _():
        for p in range(2):
            for q in range(SIDE):
                local(hid.at[p, :, pl.ds(q * piece, piece)], xp.at[p, q], r_xp.at[p])

    pl.semaphore_wait(barrier, SIDE * SIDE - 1 + 2 * SIDE)

    def send_out_proj():
        for k in range(1, SIDE * SIDE):
            t = other(k)
            col = pl.multiple_of(lax.rem(t, SIDE) * piece, 128)
            send(o.at[:, pl.ds(col, piece)], og.at[h], s_o, r_o, l, t)
        col = pl.multiple_of(j * piece, 128)
        local(o.at[:, pl.ds(col, piece)], og.at[h], r_o)

    def send_rows():
        for k in range(1, SIDE):
            jj = lax.rem(j + k, SIDE)
            col = pl.multiple_of(jj * piece, 128)
            send(o.at[:, pl.ds(col, piece)], og.at[j], s_o, r_o, l, SIDE * i + jj)
        col = pl.multiple_of(j * piece, 128)
        local(o.at[:, pl.ds(col, piece)], og.at[j], r_o)

    def send_stale():
        for k in range(1, SIDE * SIDE):
            t = other(k)
            send(st.at[t], sg.at[h], s_st, r_st, l, t)
        local(st.at[h], sg.at[h], r_st)

    send_stale()

    @pl.when(~early)
    def _():
        send_out_proj()

    @pl.when(l == 1)
    def _():
        pl.semaphore_wait(go, 1)
        send_rows()

    def start(p):
        await_bytes(xp.at[p], r_xp.at[p])
        x = xp[p].astype(jnp.float32)
        width = SIDE * piece
        mean = jnp.sum(jnp.sum(x, axis=0), axis=-1, keepdims=True) / width
        cen = x - mean[None]
        spread = jnp.sum(jnp.sum(cen * cen, axis=0), axis=-1, keepdims=True) / width
        inv = 1.0 / jnp.sqrt(spread + 1e-06)
        normed = (cen * inv[None] * (1.0 + scale[...]) + shift[...]).astype(jnp.bfloat16)
        nga[p, i, j, :, :piece] = normed[0]
        nga[p, i, j, :, piece:] = normed[1]
        ngb[p, j, i, :, :piece] = normed[2]
        ngb[p, j, i, :, piece:] = normed[3]

    def own_blocks(p):
        for k in (1, 3, 2):
            jj = lax.rem(j + k, SIDE)
            ii = lax.rem(i + k, SIDE)
            send(nga.at[p, i, j], nga.at[p, i, j], s_1a.at[p], r_1a.at[p, j], l, SIDE * i + jj)
            send(ngb.at[p, j, i], ngb.at[p, j, i], s_1b.at[p], r_1b.at[p, i], l, SIDE * ii + j)

        forward(p, i, j)

    def forward(p, isrc, jsrc):
        for k in (1, 3, 2):
            jj = lax.rem(j + k, SIDE)
            ii = lax.rem(i + k, SIDE)
            send(nga.at[p, i, jsrc], nga.at[p, i, jsrc], s_2a.at[p], r_2a.at[p, i], l, SIDE * ii + j)
            send(ngb.at[p, j, isrc], ngb.at[p, j, isrc], s_2b.at[p], r_2b.at[p, j], l, SIDE * i + jj)

    def relay(p):
        for k in (1, 3, 2):
            jj = lax.rem(j + k, SIDE)
            ii = lax.rem(i + k, SIDE)
            await_bytes(nga.at[p, i, jj], r_1a.at[p, jj])
            await_bytes(ngb.at[p, j, ii], r_1b.at[p, ii])
            forward(p, ii, jj)
        for k in range(1, SIDE):
            jj = lax.rem(j + k, SIDE)
            send(xp.at[p, jj], xr.at[p, j], s_xr.at[p], r_xr.at[p], l, SIDE * i + jj)
        local(xp.at[p, j], xr.at[p, j], r_xr.at[p])


    def settle():
        @pl.when(l == 0)
        def _():
            send_rows()

        await_bytes(w, s_w)
        await_bytes(sg, r_st)
        for c in range(2):
            old = sg[:, c].astype(jnp.float32).reshape(count * rows, hs)
            kv[c, 0] = old.astype(jnp.bfloat16)

    def project(p):
        def arrive(step, c):
            k = step + lax.div(step, 2) * (5 - 2 * step)
            ii = lax.rem(i + k, SIDE)
            jj = lax.rem(j + k, SIDE)

            @pl.when(step > 0)
            def _():
                await_bytes(nga.at[p, ii], r_2a.at[p, ii])

            left = jnp.concatenate([nga[p, ii, m].astype(jnp.float32) for m in range(SIDE)], axis=0)
            pa[ii] = jnp.dot(
                left.astype(jnp.bfloat16), w[:half], preferred_element_type=jnp.float32
            )

            @pl.when(step > 0)
            def _():
                await_bytes(ngb.at[p, jj], r_2b.at[p, jj])

            right = jnp.concatenate([ngb[p, jj, m].astype(jnp.float32) for m in range(SIDE)], axis=0)
            right = jnp.dot(
                right.astype(jnp.bfloat16), w[half:], preferred_element_type=jnp.float32
            )
            pb[jj] = right.reshape(SIDE, rows, 3 * hs)
            return c

        lax.fori_loop(0, SIDE, arrive, 0, unroll=True)

        def heads(g, c):
            out = pa[g] + pb[:, g].reshape(group, 3 * hs)
            for c in range(2):
                part = out[:, c * hs : (c + 1) * hs]
                square = jnp.mean(part * part, axis=-1, keepdims=True)
                part = part * (1.0 / jnp.sqrt(square + 1e-06)) * gain[c : c + 1, :]
                if c == 0:
                    qb[g] = part.astype(jnp.bfloat16)
                else:
                    keys = part
            values = out[:, 2 * hs :]
            kv[0, p + 1, pl.ds(pl.multiple_of(g * group, group), group)] = keys.astype(jnp.bfloat16)
            kv[1, p + 1, pl.ds(pl.multiple_of(g * group, group), group)] = values.astype(jnp.bfloat16)
            fcs[p, pl.ds(g * SIDE, SIDE), 0] = keys.reshape(SIDE, rows, hs).astype(jnp.bfloat16)
            fcs[p, pl.ds(g * SIDE, SIDE), 1] = values.reshape(SIDE, rows, hs).astype(jnp.bfloat16)
            return c

        lax.fori_loop(0, SIDE, heads, 0, unroll=True)

    def attend(p):
        def one(g):
            q = qb[g]
            dims = (((1,), (1,)), ((), ()))
            keys = kv[0, p : p + 2].reshape(2 * count * rows, hs)
            values = kv[1, p : p + 2].reshape(2 * count * rows, hs)
            weights = lax.dot_general(q, keys, dims, preferred_element_type=jnp.float32)
            weights = jnp.exp(weights * factor)
            inv = 1.0 / jnp.sum(weights, axis=-1, keepdims=True)
            probs = (weights * inv).astype(jnp.bfloat16)
            mixed = jnp.dot(probs, values, preferred_element_type=jnp.float32)
            att[p, g] = mixed.astype(jnp.bfloat16)

        for gg in (2, 1, 3, 0):
            g = lax.rem(i + gg, SIDE)
            one(g)

            @pl.when(early)
            def _():
                for k in range(1, SIDE):
                    jj = lax.rem(j + k, SIDE)
                    send(att.at[p, g], atg.at[p, SIDE * j + g], s_at.at[p], r_at.at[p], l, SIDE * i + jj)
                local(att.at[p, g], atg.at[p, SIDE * j + g], r_at.at[p])

            @pl.when(~early)
            def _():
                for k in range(1 if gg == 0 else 0, SIDE):
                    jj = lax.rem(j + k, SIDE)
                    send(att.at[p, g], atg.at[p, h], s_at.at[p], r_at.at[p], l, SIDE * g + jj)
                if gg == 0:
                    local(att.at[p, g], atg.at[p, h], r_at.at[p])

    def add_up(p, update):
        base = xr[p].astype(jnp.float32).reshape(group, piece)
        result = base + gate[j] * update
        xo[p] = result.reshape(SIDE, rows, piece).astype(jnp.bfloat16)

    def by_heads(p):
        if p == 0:
            await_bytes(og.at[pl.ds(0, SIDE)], r_o)
        weight = og[0:SIDE].reshape(SIDE * hs, piece)
        await_bytes(atg.at[p], r_at.at[p])
        for gg in (2, 1, 3, 0):
            g = lax.rem(i + gg, SIDE)
            mixed = jnp.concatenate([atg[p, SIDE * m + g] for m in range(SIDE)], axis=1)
            part = jnp.dot(mixed, weight, preferred_element_type=jnp.float32)
            if gg == 0:
                up[...] = part
            else:
                prs[p, g] = part.astype(jnp.bfloat16)
                send(prs.at[p, g], rs.at[p, i], s_rs.at[p], r_rs.at[p], l, SIDE * g + j)
        await_bytes(rs.at[p, pl.ds(0, SIDE - 1)], r_rs.at[p])
        total = up[...]
        for gg in range(1, SIDE):
            total = total + rs[p, lax.rem(i + gg, SIDE)].astype(jnp.float32)
        add_up(p, total)

    def by_tokens(p):
        if p == 0:
            await_bytes(og, r_o)
        await_bytes(atg.at[p], r_at.at[p])
        mixed = jnp.concatenate([atg[p, m] for m in range(SIDE * SIDE)], axis=1)
        weight = og[...].reshape(SIDE * SIDE * hs, piece)
        update = jnp.dot(mixed, weight, preferred_element_type=jnp.float32)
        add_up(p, update)

    def finish(p):
        await_bytes(xr.at[p], r_xr.at[p])

        @pl.when(early)
        def _():
            by_heads(p)

        @pl.when(~early)
        def _():
            by_tokens(p)

        @pl.when(l < sections - 1)
        def _():
            for k in range(SIDE):
                send(xo.at[p, k], xp.at[p, j], s_xp.at[p], r_xp.at[p], nxt, SIDE * i + k)

        for k in range(1, SIDE):
            kk = lax.rem(j + k, SIDE)
            send(xo.at[p, kk], bob.at[p, j], s_bo.at[p], r_bo.at[p], l, SIDE * i + kk)
        local(xo.at[p, j], bob.at[p, j], r_bo.at[p])

    def send_cache(p):
        for k in range(1, SIDE * SIDE):
            t = other(k)
            send(fcs.at[p, t], fcb.at[p, h], s_fc.at[p], r_fc.at[p], l, t)
        local(fcs.at[p, h], fcb.at[p, h], r_fc.at[p])

    start(0)
    own_blocks(0)
    relay(0)
    settle()

    @pl.when(odd)
    def _():
        pl.semaphore_signal(go, inc=1, device_id=(prv, h), device_id_type=MESH)

    project(0)

    attend(0)
    finish(0)

    @pl.when(l == 0)
    def _():
        pl.semaphore_signal(go, inc=1, device_id=(nxt, h), device_id_type=MESH)

    start(1)

    @pl.when(~odd)
    def _():
        pl.semaphore_wait(go, 1)

    own_blocks(1)
    relay(1)
    project(1)
    attend(1)
    send_cache(0)
    send_cache(1)
    finish(1)

    for p in range(2):
        await_bytes(fcb.at[p], r_fc.at[p])
        await_bytes(bob.at[p], r_bo.at[p])
    fc_out[...] = fcb[...]
    for p in range(2):
        for q in range(SIDE):
            bo_out[p, :, q * piece : (q + 1) * piece] = bob[p, q].astype(jnp.float32)
    most = pl.ds(0, SIDE * SIDE - 1)
    three = pl.ds(0, SIDE - 1)
    await_bytes(sg.at[most], s_st)
    for p in range(2):
        await_bytes(nga.at[p, 0, three], s_1a.at[p])
        await_bytes(ngb.at[p, 0, three], s_1b.at[p])
        await_bytes(nga.at[p, three], s_2a.at[p])
        await_bytes(ngb.at[p, three], s_2b.at[p])
        await_bytes(xr.at[p, three], s_xr.at[p])
        await_bytes(fcb.at[p, most], s_fc.at[p])
        await_bytes(bob.at[p, three], s_bo.at[p])

    @pl.when(early)
    def _():
        await_bytes(og.at[three], s_o)
        for p in range(2):
            await_bytes(atg.at[p, pl.ds(0, SIDE * (SIDE - 1))], s_at.at[p])
            await_bytes(rs.at[p, three], s_rs.at[p])

    @pl.when(~early)
    def _():
        await_bytes(og.at[most], s_o)
        for p in range(2):
            await_bytes(atg.at[p, most], s_at.at[p])

    @pl.when(l < sections - 1)
    def _():
        for p in range(2):
            await_bytes(xp.at[p], s_xp.at[p])


def body(hidden, mod_shift, mod_scale, mod_gate, norm_gain, input_proj, output_proj, stale_cache):
    patches, rows, width = hidden.shape
    hs = norm_gain.shape[2]
    count = SIDE * SIDE
    piece = width // SIDE
    half = width // 2
    bf, f32 = jnp.bfloat16, jnp.float32
    shift = mod_shift.reshape(SIDE, 1, piece)
    scale = mod_scale.reshape(SIDE, 1, piece)
    gate = mod_gate.reshape(SIDE, 1, piece)
    w = input_proj[0].transpose(1, 0, 2)
    st = stale_cache[0, 1].reshape(rows, 2, count, hs).transpose(2, 1, 0, 3)
    vmem = pl.BlockSpec(memory_space=pltpu.VMEM)
    hbm = pl.BlockSpec(memory_space=pl.ANY)
    one = pltpu.SemaphoreType.DMA
    pair = pltpu.SemaphoreType.DMA((2,))
    quad = pltpu.SemaphoreType.DMA((2, SIDE))
    bo, fc = pl.pallas_call(
        block_kernel,
        out_shape=(
            jax.ShapeDtypeStruct((patches, rows, width), f32),
            jax.ShapeDtypeStruct((patches, count, 2, rows, hs), bf),
        ),
        in_specs=[hbm] + [vmem] * 4 + [hbm] * 3,
        out_specs=(vmem, vmem),
        scratch_shapes=[
            pltpu.VMEM((patches, SIDE, rows, piece), bf),
            pltpu.VMEM((patches, SIDE, SIDE, rows, half), bf),
            pltpu.VMEM((patches, SIDE, SIDE, rows, half), bf),
            pltpu.VMEM((patches, SIDE, rows, piece), bf),
            pltpu.VMEM((count, 2, rows, hs), bf),
            pltpu.VMEM((2, patches + 1, count * rows, hs), bf),
            pltpu.VMEM((SIDE, SIDE * rows, hs), bf),
            pltpu.VMEM((count, hs, piece), bf),
            pltpu.VMEM((patches, SIDE, SIDE * rows, hs), bf),
            pltpu.VMEM((patches, count, SIDE * rows, hs), bf),
            pltpu.VMEM((patches, SIDE, rows, piece), bf),
            pltpu.VMEM((patches, SIDE, rows, piece), bf),
            pltpu.VMEM((patches, count, 2, rows, hs), bf),
            pltpu.VMEM((patches, count, 2, rows, hs), bf),
            one, one, one, one,
        ] + [pair] * 4 + [pair, quad] * 4 + [pair] * 6 + [
            pltpu.VMEM((width, 3 * hs), bf),
            one,
            pltpu.SemaphoreType.REGULAR,
            pltpu.VMEM((SIDE, SIDE * rows, 3 * hs), f32),
            pltpu.VMEM((SIDE, SIDE, rows, 3 * hs), f32),
            pltpu.VMEM((SIDE * rows, piece), f32),
            pltpu.VMEM((patches, SIDE, SIDE * rows, piece), bf),
            pltpu.VMEM((patches, SIDE, SIDE * rows, piece), bf),
            pair, pair,
        ],
        compiler_params=pltpu.CompilerParams(
            collective_id=0, has_side_effects=True, vmem_limit_bytes=56 * 1024 * 1024
        ),
    )(hidden, shift, scale, gate, norm_gain[0], w, output_proj[0], st)
    outputs = bo.astype(bf)[None]
    cache = fc.transpose(0, 3, 2, 1, 4).reshape(1, patches, rows, 2, count * hs)
    return outputs, cache


def solution(mesh):
    in_specs = (
        P(None, "seq", None),
        P("pipe", None),
        P("pipe", None),
        P("pipe", None),
        P("pipe", None, None),
        P("pipe", None, None, "seq"),
        P("pipe", "seq", None),
        P("pipe", None, "seq", None, None),
    )
    out_specs = (P("pipe", None, "seq", None), P("pipe", None, "seq", None, None))
    return jax.shard_map(body, mesh=mesh, in_specs=in_specs, out_specs=out_specs, check_vma=False)
```
